512 devices in a mesh: shot: 8 (over x, core), chan: 64 (over y, z).
Axes of the slice: x: 4, y: 4, z: 16, core: 2. Of those that a mesh axis runs over, the one named last changes fastest.
Arguments:
- traces: float32 [32, 1024, 4096], P('shot', 'chan'), may hold values from -6 to 6
- shifts: int32 [32, 1024], P('shot', 'chan'), may hold values from 0 to 1023
- aperture_lo: int32 [1024], P('chan'), may hold values from 0 to 15
- aperture_hi: int32 [1024], P('chan'), may hold values from 17 to 32
- dip_band: int32 [1024], P('chan'), may hold values from 64 to 512
Outputs:
- filtered: float32 [32, 1024, 4096], P(None, ('chan', 'shot'))
The draws below stay inside these ranges and needn't reach their ends.
All inputs are finite; a program needn't handle non-finite values.
Results may differ from the reference program's by a relative error of at most 0.0003.
Values sent between devices are 32-bit elements; how exact they have to be, the bound alone decides.
No kernel may reach another device: no remote copies, remote signals or barrier semaphores. Data moves between devices by JAX's collectives and lax.ppermute only.
A program may use at most 64 MiB of HBM per device.

```python
import jax
import jax.numpy as jnp
from jax import lax

CH_DEV = 16
NT = 4096
SHOTS = 32
CHANNELS = 1024


def place_ends(entries, stream_key, smallest, top_value):
    longest = entries.shape.index(max(entries.shape))
    spots = []
    for shift in (0, 1):
        where = [jax.random.randint(jax.random.fold_in(stream_key, axis), (), 0, length) for axis, length in enumerate(entries.shape)]
        where[longest] = (where[longest] + shift) % entries.shape[longest]
        spots.append(tuple(where))
    return entries.at[spots[0]].set(smallest).at[spots[1]].set(top_value)


def levels(stream_key, shape, cuts, low, top_value):
    def one(position, parts):
        heights = jax.random.uniform(jax.random.fold_in(jax.random.fold_in(stream_key, 6), position), (parts,), jnp.float32, low / len(cuts), top_value / len(cuts))
        return jnp.repeat(jnp.exp(heights), shape[position] // parts).reshape((-1,) + (1,) * (len(shape) - position - 1))

    factor_of = one(*cuts[0])
    for cut in cuts[1:]:
        factor_of = factor_of * one(*cut)
    return factor_of


def bell_draw(key, shape, scale, most, cuts=(), kind=jnp.bfloat16):
    values = jax.random.normal(key, shape, jnp.float32) * scale
    if len(cuts) > 0:
        values = levels(key, shape, cuts, -0.22, 0.18) * values
    return jnp.clip(values, min=-most, max=most).astype(kind)


def setup_inputs(seed: int = 0) -> dict:
    splits = jax.random.split(jax.random.key(seed), 6)
    return {
        "traces": bell_draw(splits[0], (SHOTS, CHANNELS, NT), 1.0, 6.0, ((0, 8), (1, 64)), jnp.float32),
        "shifts": place_ends(jax.random.randint(splits[1], (SHOTS, CHANNELS), 0, NT // 4), jax.random.fold_in(splits[1], 1), 0, (NT // 4) - 1).astype(jnp.int32),
        "aperture_lo": place_ends(jax.random.randint(splits[2], (CHANNELS,), 0, SHOTS // 2), jax.random.fold_in(splits[2], 1), 0, (SHOTS // 2) - 1).astype(jnp.int32),
        "aperture_hi": place_ends(jax.random.randint(splits[3], (CHANNELS,), SHOTS // 2 + 1, SHOTS + 1), jax.random.fold_in(splits[3], 1), SHOTS // 2 + 1, SHOTS).astype(jnp.int32),
        "dip_band": place_ends(jax.random.randint(splits[4], (CHANNELS,), NT // 64, NT // 8 + 1), jax.random.fold_in(splits[4], 1), NT // 64, (NT // 8 + 1) - 1).astype(jnp.int32),
    }


def median_channels(signal):
    padded = jnp.pad(signal, ((5, 5), (0, 0)))
    count = signal.shape[0]
    stacked = jnp.stack([padded[offset:offset + count] for offset in range(11)])
    return jnp.sort(stacked, axis=0)[5]


def clean_shot(packed):
    trace_block, shift_row = packed
    samples_ids = jnp.arange(NT, dtype=jnp.int32)
    source = samples_ids[None, :] + shift_row[:, None]
    picked = jnp.take_along_axis(trace_block, jnp.minimum(source, NT - 1).astype(jnp.int32), axis=1)
    aligned = jnp.where(source < NT, picked, jnp.zeros_like(picked))
    first_pass = aligned - median_channels(aligned)
    second_pass = first_pass - median_channels(first_pass)
    backward = samples_ids[None, :] - shift_row[:, None]
    picked_back = jnp.take_along_axis(second_pass, jnp.maximum(backward, 0).astype(jnp.int32), axis=1)
    return jnp.where(backward >= 0, picked_back, jnp.zeros_like(picked_back))


def reference(traces, shifts, aperture_lo, aperture_hi, dip_band):
    upgoing = lax.map(clean_shot, (traces, shifts))
    shot_ids = jnp.arange(SHOTS, dtype=jnp.int32)
    in_aperture = (shot_ids[:, None] >= aperture_lo[None, :]) & (shot_ids[:, None] < aperture_hi[None, :])
    upgoing = jnp.where(in_aperture[:, :, None], upgoing, jnp.zeros_like(upgoing))
    wave_ids = jnp.arange(SHOTS, dtype=jnp.int32)
    wave_abs = jnp.abs(jnp.where(wave_ids < SHOTS // 2, wave_ids, wave_ids - SHOTS))
    freq_ids = jnp.arange(NT, dtype=jnp.int32)
    freq_abs = jnp.abs(jnp.where(freq_ids < NT // 2, freq_ids, freq_ids - NT))
    block_count = CHANNELS // CH_DEV
    grouped = upgoing.reshape(SHOTS, block_count, CH_DEV, NT).transpose(1, 0, 2, 3)
    band_blocks = dip_band.reshape(block_count, CH_DEV)

    def filter_group(packed):
        gathered, band_rows = packed
        spectrum = jnp.fft.fft2(gathered, axes=(0, 2))
        pass_mask = (wave_abs[:, None, None] * band_rows[None, :, None]) <= freq_abs[None, None, :]
        spectrum = jnp.where(pass_mask, spectrum, jnp.zeros_like(spectrum))
        return jnp.real(jnp.fft.ifft2(spectrum, axes=(0, 2)))

    result = lax.map(filter_group, (grouped, band_blocks))
    return result.transpose(1, 0, 2, 3).reshape(SHOTS, CHANNELS, NT)
```

```python
import functools

import jax
import jax.numpy as jnp
import numpy as np
from jax import lax
from jax.experimental import pallas as pl
from jax.experimental.pallas import tpu as pltpu
from jax.sharding import PartitionSpec as P

LANES = 128
HALF = 5
HALO = 2 * HALF
HIGHEST = lax.Precision.HIGHEST


def whole(space=pltpu.VMEM):
    return pl.BlockSpec(memory_space=space)


def align_kernel(dims, shifts_ref, traces_ref, down_ref, up_ref, held, sems):
    shots, chans, rows = dims
    tiles = chans * rows
    for shot in range(shots):
        pltpu.make_async_copy(
            traces_ref.at[pl.ds(shot * tiles, tiles)], held.at[pl.ds(shot * tiles, tiles)], sems.at[shot]
        ).start()
    held[pl.ds(shots * tiles, held.shape[0] - shots * tiles), :] = jnp.zeros(
        (held.shape[0] - shots * tiles, LANES), jnp.float32
    )
    lane = lax.broadcasted_iota(jnp.int32, (rows, LANES), 1)
    sample = lax.broadcasted_iota(jnp.int32, (rows, LANES), 0) * LANES + lane
    for shot in range(shots):
        pltpu.make_async_copy(
            traces_ref.at[pl.ds(shot * tiles, tiles)], held.at[pl.ds(shot * tiles, tiles)], sems.at[shot]
        ).wait()
    for shot in range(shots):
        for chan in range(chans):
            shift = shifts_ref[shot, chan]
            whole_rows, part = shift // LANES, shift % LANES
            base = shot * tiles + (chan // 8) * (rows * 8) + chan % 8
            first = held[pl.ds(base + whole_rows * 8, rows, stride=8), :]
            second = held[pl.ds(base + whole_rows * 8 + 8, rows, stride=8), :]
            mixed = jnp.where(lane >= part, first, second)
            moved = pltpu.roll(mixed, (LANES - part) % LANES, 1)
            moved = jnp.where(sample < rows * LANES - shift, moved, 0.0)
            if chan < HALO:
                down_ref[shot, chan] = moved
            if chan >= chans - HALO:
                up_ref[shot, chan - (chans - HALO)] = moved


def align(traces, shifts):
    shots, chans, length = traces.shape
    rows = length // LANES
    flat = traces.reshape(shots, chans // 8, 8, rows, LANES).transpose(0, 1, 3, 2, 4).reshape(-1, LANES)
    edge = jax.ShapeDtypeStruct((shots, HALO, rows, LANES), jnp.float32)
    pad = 8 * 9
    return pl.pallas_call(
        functools.partial(align_kernel, (shots, chans, rows)),
        out_shape=(edge, edge),
        in_specs=[whole(pltpu.SMEM), whole(pl.ANY)],
        out_specs=(whole(), whole()),
        scratch_shapes=[
            pltpu.VMEM((shots * chans * rows + pad, LANES), jnp.float32),
            pltpu.SemaphoreType.DMA((shots,)),
        ],
        name="align",
    )(shifts, flat)


def order(a, b):
    return jnp.minimum(a, b), jnp.maximum(a, b)


def medians(values, count):
    total = len(values)
    pairs = {}
    blocks = {}

    def pair(start):
        if start not in pairs:
            pairs[start] = order(values[start], values[start + 1])
        return pairs[start]

    def block(start):
        if start not in blocks:
            (a, b), (c, d) = pair(start), pair(start + 2)
            low, m = order(a, c)
            n, high = order(b, d)
            m, n = order(m, n)
            blocks[start] = (low, m, n, high)
        return blocks[start]

    result = []
    for group in range(-1, (count + 3) // 4):
        wanted = [w for w in range(4 * group + 1, 4 * group + 5) if 0 <= w < count]
        if not wanted:
            continue
        a1, a2, a3, a4 = block(4 * group + 4)
        b1, b2, b3, b4 = block(4 * group + 8)
        t, u = jnp.maximum(a1, b1), jnp.minimum(a3, b3)
        c4 = jnp.maximum(a3, b3)
        c2, c3 = order(t, u)
        d1 = jnp.minimum(a2, b2)
        t, u = jnp.maximum(a2, b2), jnp.minimum(a4, b4)
        d2, d3 = order(t, u)
        m3, (m4, m5), m6 = jnp.maximum(d1, c2), order(d2, c3), jnp.minimum(d3, c4)
        for half, extra in ((0, 4 * group + 2), (1, 4 * group + 12)):
            mine = [w for w in wanted if (w - 4 * group - 1) // 2 == half]
            if not mine:
                continue
            p, q = pair(extra)
            s5 = jnp.minimum(m5, jnp.minimum(jnp.maximum(m4, p), jnp.maximum(m3, q)))
            s6 = jnp.minimum(m6, jnp.minimum(jnp.maximum(m5, p), jnp.maximum(m4, q)))
            for w in mine:
                lone = extra - 1 if (w - 4 * group - 1) == 0 else extra + 2 if (w - 4 * group - 1) == 3 else (
                    4 * group + 12 if half == 0 else 4 * group + 3
                )
                assert w <= lone <= w + 10 and lone < total
                result.append(jnp.maximum(s5, jnp.minimum(s6, values[lone])))
    assert len(result) == count
    return result


def clean_kernel(dims, shifts_ref, low_ref, high_ref, left_ref, down_ref, up_ref, right_ref, out_ref, held):
    shots, chans, rows = dims
    first_shot = lax.axis_index("shot") * shots
    lead = 8
    for chan in range(chans):
        held[chan, pl.ds(0, lead), :] = jnp.zeros((lead, LANES), jnp.float32)
    lane = lax.broadcasted_iota(jnp.int32, (rows, LANES), 1)

    def one_shot(shot, carry):
        def one_part(part, inner):
            place = pl.ds(pl.multiple_of(part * 8, 8), 8)
            values = [left_ref[shot, i, place, :] for i in range(HALO)]
            values += [down_ref[shot, i, place, :] for i in range(HALO)]
            values += [up_ref[shot, i, place, :] for i in range(2 * HALO - chans, HALO)]
            values += [right_ref[shot, i, place, :] for i in range(HALO)]
            once = medians(values, chans + HALO)
            once = [values[HALF + i] - once[i] for i in range(chans + HALO)]
            twice = medians(once, chans)
            stored = pl.ds(pl.multiple_of(lead + part * 8, 8), 8)
            for i in range(chans):
                held[i, stored, :] = once[HALF + i] - twice[i]
            return inner

        lax.fori_loop(0, rows // 8, one_part, 0)
        for chan in range(chans):
            shift = shifts_ref[shot, chan]
            whole_rows, part = shift // LANES, shift % LANES
            inside = (first_shot + shot >= low_ref[chan]) & (first_shot + shot < high_ref[chan])
            first = held[chan, pl.ds(lead - whole_rows, rows), :]
            second = held[chan, pl.ds(lead - 1 - whole_rows, rows), :]
            mixed = jnp.where(lane < LANES - part, first, second)
            moved = pltpu.roll(mixed, part, 1)
            out_ref[chan // 2, shot, chan % 2] = jnp.where(inside, moved, 0.0)
        return carry

    lax.fori_loop(0, shots, one_shot, 0)


def clean(shifts, low, high, left, down, up, right, chans, groups):
    shots, _, rows, _ = down.shape
    return pl.pallas_call(
        functools.partial(clean_kernel, (shots, chans, rows)),
        out_shape=jax.ShapeDtypeStruct((groups, shots, chans // groups, rows, LANES), jnp.float32),
        in_specs=[whole(pltpu.SMEM)] * 3 + [whole()] * 4,
        out_specs=whole(),
        scratch_shapes=[pltpu.VMEM((chans, 8 + rows, LANES), jnp.float32)],
        name="clean",
    )(shifts, low, high, left, down, up, right)


def real_forward(x):
    n = len(x)
    if n == 1:
        return [(x[0], None)]
    if n == 2:
        return [(x[0] + x[1], None), (x[0] - x[1], None)]
    even, odd = real_forward(x[0::2]), real_forward(x[1::2])
    out = [None] * (n // 2 + 1)
    for k in range(n // 4 + 1):
        (er, ei), (or_, oi) = even[k], odd[k]
        if k == 0:
            out[0] = (er + or_, None)
            out[n // 2] = (er - or_, None)
        elif 4 * k == n:
            out[k] = (er, -or_)
        else:
            c, s = math_cos(k, n), math_sin(k, n)
            tr, ti = or_ * c + oi * s, oi * c - or_ * s
            out[k] = (er + tr, ei + ti)
            out[n // 2 - k] = (er - tr, ti - ei)
    return out


def real_backward(spectrum, n):
    if n == 1:
        return [spectrum[0][0]]
    if n == 2:
        return [spectrum[0][0] + spectrum[1][0], spectrum[0][0] - spectrum[1][0]]
    even, odd = [None] * (n // 4 + 1), [None] * (n // 4 + 1)
    for k in range(n // 4 + 1):
        (ar, ai), (br, bi) = spectrum[k], spectrum[n // 2 - k]
        if k == 0:
            even[0], odd[0] = (ar + br, None), (ar - br, None)
        elif 4 * k == n:
            even[k], odd[k] = (ar + ar, None), (-(ai + ai), None)
        else:
            c, s = math_cos(k, n), math_sin(k, n)
            even[k] = (ar + br, ai - bi)
            dr, di = ar - br, ai + bi
            odd[k] = (dr * c - di * s, di * c + dr * s)
    first, second = real_backward(even, n // 2), real_backward(odd, n // 2)
    return [v for both in zip(first, second) for v in both]


def math_cos(k, n):
    return float(np.float32(np.cos(2 * np.pi * k / n)))


def math_sin(k, n):
    return float(np.float32(np.sin(2 * np.pi * k / n)))


def tables(shots, rows):
    a = np.arange(rows)
    outer = 2 * np.pi * (np.outer(a, a) % rows) / rows
    b = np.arange(LANES)
    inner = 2 * np.pi * (np.outer(b, b) % LANES) / LANES
    turn = 2 * np.pi * np.outer(a, b) / (rows * LANES)
    c, s = np.cos(outer), np.sin(outer)
    outer_forward = np.block([[c, s], [-s, c]])
    outer_backward = np.block([[c, -s], [s, c]])
    c, s = np.cos(inner), np.sin(inner)
    inner_forward = np.block([[c, -s], [s, c]])
    inner_backward = np.block([[c, s], [-s, c]]) / (shots * rows * LANES)
    twist = np.stack([np.cos(turn), np.sin(turn)])
    return [jnp.asarray(t, jnp.float32) for t in (outer_forward, outer_backward, inner_forward, inner_backward, twist)]


def dip_kernel(dims, bands_ref, data_ref, outer_f, outer_b, inner_f, inner_b, twist_ref, out_ref, held):
    shots, recs, rows = dims
    high = shots // 2
    first_rec = lax.axis_index("shot") * recs
    lane = lax.broadcasted_iota(jnp.int32, (rows, LANES), 1)
    frequency = lax.broadcasted_iota(jnp.int32, (rows, LANES), 0) + rows * lane
    distance = jnp.minimum(frequency, rows * LANES - frequency)

    for rec in range(recs):
        lanes = pl.ds(rec * LANES, LANES)

        def shots_forward(part, carry):
            place = pl.ds(pl.multiple_of(part * 8, 8), 8)
            below = pl.ds(pl.multiple_of(rows + part * 8, 8), 8)
            out = real_forward([data_ref[shot, rec, place, :] for shot in range(shots)])
            for k in range(high + 1):
                re, im = out[k]
                held[k, place, lanes] = re
                if k > 0:
                    held[k, below, lanes] = jnp.zeros_like(re) if im is None else im
            return carry

        lax.fori_loop(0, rows // 8, shots_forward, 0)

    def one_wave(k, carry):
        spec = jnp.dot(outer_f[...], held[k], precision=HIGHEST, preferred_element_type=jnp.float32)
        cos, sin = twist_ref[0], twist_ref[1]
        lines = []
        for rec in range(recs):
            re, im = spec[:rows, rec * LANES : (rec + 1) * LANES], spec[rows:, rec * LANES : (rec + 1) * LANES]
            lines.append(jnp.concatenate([re * cos + im * sin, im * cos - re * sin], axis=1))
        wave = jnp.concatenate(lines, axis=0)
        wave = jnp.dot(wave, inner_f[...], precision=HIGHEST, preferred_element_type=jnp.float32)
        keep = [distance >= k * bands_ref[first_rec + rec] for rec in range(recs)]
        keep = jnp.concatenate([jnp.concatenate([one, one], axis=1) for one in keep], axis=0)
        wave = jnp.where(keep, wave, 0.0)
        wave = jnp.dot(wave, inner_b[...], precision=HIGHEST, preferred_element_type=jnp.float32)
        res, ims = [], []
        for rec in range(recs):
            re, im = wave[rec * rows : (rec + 1) * rows, :LANES], wave[rec * rows : (rec + 1) * rows, LANES:]
            res.append(re * cos - im * sin)
            ims.append(im * cos + re * sin)
        back = jnp.concatenate([jnp.concatenate(res, axis=1), jnp.concatenate(ims, axis=1)], axis=0)
        held[k] = jnp.dot(outer_b[...], back, precision=HIGHEST, preferred_element_type=jnp.float32)
        return carry

    lax.fori_loop(1, high + 1, one_wave, 0)

    for rec in range(recs):
        lanes = pl.ds(rec * LANES, LANES)

        def shots_backward(part, carry):
            place = pl.ds(pl.multiple_of(part * 8, 8), 8)
            below = pl.ds(pl.multiple_of(rows + part * 8, 8), 8)
            spectrum = [(held[0, place, lanes] * (1.0 / shots), None)]
            for k in range(1, high + 1):
                spectrum.append((held[k, place, lanes], held[k, below, lanes] if k < high else None))
            back = real_backward(spectrum, shots)
            for shot in range(shots):
                out_ref[shot, pl.ds(part * (8 * recs) + rec, 8, stride=recs), :] = back[shot]
            return carry

        lax.fori_loop(0, rows // 8, shots_backward, 0)


def dip_filter(gathered, dip_band):
    shots, recs, rows, _ = gathered.shape
    out = pl.pallas_call(
        functools.partial(dip_kernel, (shots, recs, rows)),
        out_shape=jax.ShapeDtypeStruct((shots, rows * recs, LANES), jnp.float32),
        in_specs=[whole(pltpu.SMEM)] + [whole()] * 6,
        out_specs=whole(),
        scratch_shapes=[pltpu.VMEM((shots // 2 + 1, 2 * rows, recs * LANES), jnp.float32)],
        name="dip",
    )(dip_band, gathered, *tables(shots, rows))
    return out.reshape(shots, rows, recs, LANES).transpose(0, 2, 1, 3).reshape(shots, recs, rows * LANES)


def local(traces, shifts, aperture_lo, aperture_hi, dip_band):
    shots, chans, length = traces.shape
    blocks, groups = lax.axis_size("chan"), lax.axis_size("shot")
    down, up = align(traces, shifts)
    left = lax.ppermute(up, "chan", [(i, i + 1) for i in range(blocks - 1)])
    right = lax.ppermute(down, "chan", [(i + 1, i) for i in range(blocks - 1)])
    parted = clean(shifts, aperture_lo, aperture_hi, left, down, up, right, chans, groups)
    arrived = lax.all_to_all(parted, "shot", split_axis=0, concat_axis=0, tiled=True)
    gathered = arrived.reshape(groups * shots, chans // groups, length // LANES, LANES)
    return dip_filter(gathered, dip_band)


def solution(mesh):
    return jax.shard_map(
        local,
        mesh=mesh,
        in_specs=(P("shot", "chan", None), P("shot", "chan"), P("chan"), P("chan"), P("chan")),
        out_specs=P(None, ("chan", "shot"), None),
        check_vma=False,
    )
```

```python
import functools

import jax
import jax.numpy as jnp
import numpy as np
from jax import lax
from jax.experimental import pallas as pl
from jax.experimental.pallas import tpu as pltpu
from jax.sharding import PartitionSpec as P

LANES = 128
HALF = 5
HALO = 2 * HALF
GRANT = 16 << 20
WAVES = 4


def whole(space=pltpu.VMEM):
    return pl.BlockSpec(memory_space=space)


def align_kernel(dims, shifts_ref, traces_ref, down_ref, up_ref, held, sems):
    shots, chans, rows = dims
    tiles = chans * rows
    for shot in range(shots):
        pltpu.make_async_copy(
            traces_ref.at[pl.ds(shot * tiles, tiles)], held.at[pl.ds(shot * tiles, tiles)], sems.at[shot]
        ).start()
    held[pl.ds(shots * tiles, held.shape[0] - shots * tiles), :] = jnp.zeros(
        (held.shape[0] - shots * tiles, LANES), jnp.float32
    )
    lane = lax.broadcasted_iota(jnp.int32, (rows, LANES), 1)
    sample = lax.broadcasted_iota(jnp.int32, (rows, LANES), 0) * LANES + lane
    for shot in range(shots):
        pltpu.make_async_copy(
            traces_ref.at[pl.ds(shot * tiles, tiles)], held.at[pl.ds(shot * tiles, tiles)], sems.at[shot]
        ).wait()
    for shot in range(shots):
        for chan in range(chans):
            shift = shifts_ref[shot, chan]
            whole_rows, part = shift // LANES, shift % LANES
            base = shot * tiles + (chan // 8) * (rows * 8) + chan % 8
            first = held[pl.ds(base + whole_rows * 8, rows, stride=8), :]
            second = held[pl.ds(base + whole_rows * 8 + 8, rows, stride=8), :]
            mixed = jnp.where(lane >= part, first, second)
            moved = pltpu.roll(mixed, (LANES - part) % LANES, 1)
            moved = jnp.where(sample < rows * LANES - shift, moved, 0.0)
            if chan < HALO:
                down_ref[shot, chan] = moved
            if chan >= chans - HALO:
                up_ref[shot, chan - (chans - HALO)] = moved


def align(traces, shifts):
    shots, chans, length = traces.shape
    rows = length // LANES
    flat = traces.reshape(shots, chans // 8, 8, rows, LANES).transpose(0, 1, 3, 2, 4).reshape(-1, LANES)
    edge = jax.ShapeDtypeStruct((shots, HALO, rows, LANES), jnp.float32)
    pad = 8 * 9
    return pl.pallas_call(
        functools.partial(align_kernel, (shots, chans, rows)),
        out_shape=(edge, edge),
        in_specs=[whole(pltpu.SMEM), whole(pl.ANY)],
        out_specs=(whole(), whole()),
        scratch_shapes=[
            pltpu.VMEM((shots * chans * rows + pad, LANES), jnp.float32),
            pltpu.SemaphoreType.DMA((shots,)),
        ],
        compiler_params=pltpu.CompilerParams(vmem_limit_bytes=GRANT),
        name="align",
    )(shifts, flat)


def order(a, b):
    return jnp.minimum(a, b), jnp.maximum(a, b)


def medians(values, count):
    total = len(values)
    pairs = {}
    blocks = {}

    def pair(start):
        if start not in pairs:
            pairs[start] = order(values[start], values[start + 1])
        return pairs[start]

    def block(start):
        if start not in blocks:
            (a, b), (c, d) = pair(start), pair(start + 2)
            low, m = order(a, c)
            n, high = order(b, d)
            m, n = order(m, n)
            blocks[start] = (low, m, n, high)
        return blocks[start]

    result = []
    for group in range(-1, (count + 3) // 4):
        wanted = [w for w in range(4 * group + 1, 4 * group + 5) if 0 <= w < count]
        if not wanted:
            continue
        a1, a2, a3, a4 = block(4 * group + 4)
        b1, b2, b3, b4 = block(4 * group + 8)
        t, u = jnp.maximum(a1, b1), jnp.minimum(a3, b3)
        c4 = jnp.maximum(a3, b3)
        c2, c3 = order(t, u)
        d1 = jnp.minimum(a2, b2)
        t, u = jnp.maximum(a2, b2), jnp.minimum(a4, b4)
        d2, d3 = order(t, u)
        m3, (m4, m5), m6 = jnp.maximum(d1, c2), order(d2, c3), jnp.minimum(d3, c4)
        for half, extra in ((0, 4 * group + 2), (1, 4 * group + 12)):
            mine = [w for w in wanted if (w - 4 * group - 1) // 2 == half]
            if not mine:
                continue
            p, q = pair(extra)
            s5 = jnp.minimum(m5, jnp.minimum(jnp.maximum(m4, p), jnp.maximum(m3, q)))
            s6 = jnp.minimum(m6, jnp.minimum(jnp.maximum(m5, p), jnp.maximum(m4, q)))
            for w in mine:
                lone = extra - 1 if (w - 4 * group - 1) == 0 else extra + 2 if (w - 4 * group - 1) == 3 else (
                    4 * group + 12 if half == 0 else 4 * group + 3
                )
                assert w <= lone <= w + 10 and lone < total
                result.append(jnp.maximum(s5, jnp.minimum(s6, values[lone])))
    assert len(result) == count
    return result


def clean_kernel(dims, shifts_ref, low_ref, high_ref, left_ref, down_ref, up_ref, right_ref, out_ref, held):
    shots, chans, rows = dims
    first_shot = lax.axis_index("shot") * shots
    lead = 8
    for chan in range(chans):
        held[chan, pl.ds(0, lead), :] = jnp.zeros((lead, LANES), jnp.float32)
    lane = lax.broadcasted_iota(jnp.int32, (rows, LANES), 1)

    def one_shot(shot, carry):
        def one_part(part, inner):
            place = pl.ds(pl.multiple_of(part * 8, 8), 8)
            values = [left_ref[shot, i, place, :] for i in range(HALO)]
            values += [down_ref[shot, i, place, :] for i in range(HALO)]
            values += [up_ref[shot, i, place, :] for i in range(2 * HALO - chans, HALO)]
            values += [right_ref[shot, i, place, :] for i in range(HALO)]
            once = medians(values, chans + HALO)
            once = [values[HALF + i] - once[i] for i in range(chans + HALO)]
            twice = medians(once, chans)
            stored = pl.ds(pl.multiple_of(lead + part * 8, 8), 8)
            for i in range(chans):
                held[i, stored, :] = once[HALF + i] - twice[i]
            return inner

        lax.fori_loop(0, rows // 8, one_part, 0)
        for chan in range(chans):
            shift = shifts_ref[shot, chan]
            whole_rows, part = shift // LANES, shift % LANES
            inside = (first_shot + shot >= low_ref[chan]) & (first_shot + shot < high_ref[chan])
            first = held[chan, pl.ds(lead - whole_rows, rows), :]
            second = held[chan, pl.ds(lead - 1 - whole_rows, rows), :]
            mixed = jnp.where(lane < LANES - part, first, second)
            moved = pltpu.roll(mixed, part, 1)
            out_ref[chan // 2, shot, chan % 2] = jnp.where(inside, moved, 0.0)
        return carry

    lax.fori_loop(0, shots, one_shot, 0)


def clean(shifts, low, high, left, down, up, right, chans, groups):
    shots, _, rows, _ = down.shape
    return pl.pallas_call(
        functools.partial(clean_kernel, (shots, chans, rows)),
        out_shape=jax.ShapeDtypeStruct((groups, shots, chans // groups, rows, LANES), jnp.float32),
        in_specs=[whole(pltpu.SMEM)] * 3 + [whole()] * 4,
        out_specs=whole(),
        scratch_shapes=[pltpu.VMEM((chans, 8 + rows, LANES), jnp.float32)],
        compiler_params=pltpu.CompilerParams(vmem_limit_bytes=GRANT),
        name="clean",
    )(shifts, low, high, left, down, up, right)


def real_forward(x):
    n = len(x)
    if n == 1:
        return [(x[0], None)]
    if n == 2:
        return [(x[0] + x[1], None), (x[0] - x[1], None)]
    even, odd = real_forward(x[0::2]), real_forward(x[1::2])
    out = [None] * (n // 2 + 1)
    for k in range(n // 4 + 1):
        (er, ei), (or_, oi) = even[k], odd[k]
        if k == 0:
            out[0] = (er + or_, None)
            out[n // 2] = (er - or_, None)
        elif 4 * k == n:
            out[k] = (er, -or_)
        else:
            c, s = math_cos(k, n), math_sin(k, n)
            tr, ti = or_ * c + oi * s, oi * c - or_ * s
            out[k] = (er + tr, ei + ti)
            out[n // 2 - k] = (er - tr, ti - ei)
    return out


def real_backward(spectrum, n):
    if n == 1:
        return [spectrum[0][0]]
    if n == 2:
        return [spectrum[0][0] + spectrum[1][0], spectrum[0][0] - spectrum[1][0]]
    even, odd = [None] * (n // 4 + 1), [None] * (n // 4 + 1)
    for k in range(n // 4 + 1):
        (ar, ai), (br, bi) = spectrum[k], spectrum[n // 2 - k]
        if k == 0:
            even[0], odd[0] = (ar + br, None), (ar - br, None)
        elif 4 * k == n:
            even[k], odd[k] = (ar + ar, None), (-(ai + ai), None)
        else:
            c, s = math_cos(k, n), math_sin(k, n)
            even[k] = (ar + br, ai - bi)
            dr, di = ar - br, ai + bi
            odd[k] = (dr * c - di * s, di * c + dr * s)
    first, second = real_backward(even, n // 2), real_backward(odd, n // 2)
    return [v for both in zip(first, second) for v in both]


def math_cos(k, n):
    return float(np.float32(np.cos(2 * np.pi * k / n)))


def math_sin(k, n):
    return float(np.float32(np.sin(2 * np.pi * k / n)))


def split(x):
    top = x.astype(jnp.bfloat16)
    return top, (x - top.astype(jnp.float32)).astype(jnp.bfloat16)


def constant_split(x):
    x = np.asarray(x, np.float32)
    top = x.astype(jnp.bfloat16)
    return top, (x - top.astype(np.float32)).astype(jnp.bfloat16)


def tables(shots, rows):
    a = np.arange(rows)
    outer = 2 * np.pi * (np.outer(a, a) % rows) / rows
    b = np.arange(LANES)
    inner = 2 * np.pi * (np.outer(b, b) % LANES) / LANES
    turn = 2 * np.pi * np.outer(a, b) / (rows * LANES)
    c, s = np.cos(outer), np.sin(outer)
    outer_forward = np.block([[c, s], [-s, c]])
    outer_backward = np.block([[c, -s], [s, c]])
    c, s = np.cos(inner), np.sin(inner)
    inner_forward = np.block([[c, -s], [s, c]])
    inner_backward = np.block([[c, s], [-s, c]]) / (shots * rows * LANES)
    left = []
    for matrix in (outer_forward, outer_backward):
        top, rest = constant_split(matrix)
        left.append(jnp.asarray(np.concatenate([top, top, rest], axis=1)))
    right = []
    for matrix in (inner_forward, inner_backward):
        top, rest = constant_split(matrix)
        right.append(jnp.asarray(np.concatenate([top, top, rest], axis=0)))
    twist = jnp.asarray(np.stack([np.cos(turn), np.sin(turn)]), jnp.float32)
    return (*left, *right, twist)


def dot(a, b):
    return jnp.dot(a, b, preferred_element_type=jnp.float32)


def dip_kernel(dims, bands_ref, data_ref, outer_f, outer_b, inner_f, inner_b, twist_ref, out_ref, held):
    shots, recs, rows = dims
    high = shots // 2
    first_rec = lax.axis_index("shot") * recs
    lane = lax.broadcasted_iota(jnp.int32, (rows, LANES), 1)
    frequency = lax.broadcasted_iota(jnp.int32, (rows, LANES), 0) + rows * lane
    distance = jnp.minimum(frequency, rows * LANES - frequency)

    for rec in range(recs):
        lanes = pl.ds(rec * LANES, LANES)

        def shots_forward(part, carry):
            place = pl.ds(pl.multiple_of(part * 8, 8), 8)
            below = pl.ds(pl.multiple_of(rows + part * 8, 8), 8)
            out = real_forward([data_ref[shot, rec, place, :] for shot in range(shots)])
            for k in range(high + 1):
                re, im = out[k]
                held[k, place, lanes] = re
                if k > 0:
                    held[k, below, lanes] = jnp.zeros_like(re) if im is None else im
            return carry

        lax.fori_loop(0, rows // 8, shots_forward, 0)

    def left_product(matrix, k):
        top, rest = split(held[k])
        return dot(matrix[...], jnp.concatenate([top, rest, top], axis=0))

    def right_product(lines, matrix):
        top, rest = split(lines)
        return dot(jnp.concatenate([top, rest, top], axis=1), matrix[...])

    def some_waves(step, carry):
        cos, sin = twist_ref[0], twist_ref[1]
        first = 1 + step * WAVES
        lines = []
        for i in range(WAVES):
            spec = left_product(outer_f, first + i)
            for rec in range(recs):
                mine = slice(rec * LANES, (rec + 1) * LANES)
                re, im = spec[:rows, mine], spec[rows:, mine]
                lines.append(jnp.concatenate([re * cos + im * sin, im * cos - re * sin], axis=1))
        wave = right_product(jnp.concatenate(lines, axis=0), inner_f)
        kept = []
        for i in range(WAVES):
            for rec in range(recs):
                n = (i * recs + rec) * rows
                keep = distance >= (first + i) * bands_ref[first_rec + rec]
                kept.append(
                    jnp.concatenate(
                        [
                            jnp.where(keep, wave[n : n + rows, :LANES], 0.0),
                            jnp.where(keep, wave[n : n + rows, LANES:], 0.0),
                        ],
                        axis=1,
                    )
                )
        wave = right_product(jnp.concatenate(kept, axis=0), inner_b)
        for i in range(WAVES):
            for rec in range(recs):
                n = (i * recs + rec) * rows
                lanes = slice(rec * LANES, (rec + 1) * LANES)
                re, im = wave[n : n + rows, :LANES], wave[n : n + rows, LANES:]
                held[first + i, :rows, lanes] = re * cos - im * sin
                held[first + i, rows:, lanes] = im * cos + re * sin
        for i in range(WAVES):
            held[first + i] = left_product(outer_b, first + i)
        return carry

    lax.fori_loop(0, high // WAVES, some_waves, 0)

    for rec in range(recs):
        lanes = pl.ds(rec * LANES, LANES)

        def shots_backward(part, carry):
            place = pl.ds(pl.multiple_of(part * 8, 8), 8)
            below = pl.ds(pl.multiple_of(rows + part * 8, 8), 8)
            spectrum = [(held[0, place, lanes] * (1.0 / shots), None)]
            for k in range(1, high + 1):
                spectrum.append((held[k, place, lanes], held[k, below, lanes] if k < high else None))
            back = real_backward(spectrum, shots)
            for shot in range(shots):
                out_ref[shot, pl.ds(part * (8 * recs) + rec, 8, stride=recs), :] = back[shot]
            return carry

        lax.fori_loop(0, rows // 8, shots_backward, 0)


def dip_filter(gathered, dip_band):
    shots, recs, rows, _ = gathered.shape
    out = pl.pallas_call(
        functools.partial(dip_kernel, (shots, recs, rows)),
        out_shape=jax.ShapeDtypeStruct((shots, rows * recs, LANES), jnp.float32),
        in_specs=[whole(pltpu.SMEM)] + [whole()] * 6,
        out_specs=whole(),
        scratch_shapes=[pltpu.VMEM((shots // 2 + 1, 2 * rows, recs * LANES), jnp.float32)],
        compiler_params=pltpu.CompilerParams(vmem_limit_bytes=GRANT),
        name="dip",
    )(dip_band, gathered, *tables(shots, rows))
    return out.reshape(shots, rows, recs, LANES).transpose(0, 2, 1, 3).reshape(shots, recs, rows * LANES)


def local(traces, shifts, aperture_lo, aperture_hi, dip_band):
    shots, chans, length = traces.shape
    blocks, groups = lax.axis_size("chan"), lax.axis_size("shot")
    down, up = align(traces, shifts)
    left = lax.ppermute(up, "chan", [(i, i + 1) for i in range(blocks - 1)])
    right = lax.ppermute(down, "chan", [(i + 1, i) for i in range(blocks - 1)])
    parted = clean(shifts, aperture_lo, aperture_hi, left, down, up, right, chans, groups)
    arrived = lax.all_to_all(parted, "shot", split_axis=0, concat_axis=0, tiled=True)
    gathered = arrived.reshape(groups * shots, chans // groups, length // LANES, LANES)
    return dip_filter(gathered, dip_band)


def solution(mesh):
    return jax.shard_map(
        local,
        mesh=mesh,
        in_specs=(P("shot", "chan", None), P("shot", "chan"), P("chan"), P("chan"), P("chan")),
        out_specs=P(None, ("chan", "shot"), None),
        check_vma=False,
    )
```

```python
import functools

import jax
import jax.numpy as jnp
import numpy as np
from jax import lax
from jax.experimental import pallas as pl
from jax.experimental.pallas import tpu as pltpu
from jax.sharding import PartitionSpec as P

LANES = 128
HALF = 5
HALO = 2 * HALF
TAIL = 8 * 9
GRANT = 16 << 20
WAVES = 16


def whole(space=pltpu.VMEM):
    return pl.BlockSpec(memory_space=space)


def align_kernel(dims, shifts_ref, traces_ref, down_ref, up_ref, held, shifts, shift_sem, sems):
    shots, chans, rows = dims
    tiles = chans * rows
    count = pltpu.make_async_copy(shifts_ref, shifts, shift_sem)
    count.start()
    copies = []
    for shot in range(shots):
        source, target = traces_ref.at[pl.ds(shot * tiles, tiles)], held.at[shot, pl.ds(0, tiles)]
        copies.append(pltpu.make_async_copy(source, target, sems.at[shot]))
        copies[-1].start()
        held[shot, pl.ds(tiles, TAIL), :] = jnp.zeros((TAIL, LANES), jnp.float32)
    lane = lax.broadcasted_iota(jnp.int32, (rows, LANES), 1)
    sample = lax.broadcasted_iota(jnp.int32, (rows, LANES), 0) * LANES + lane
    count.wait()
    for shot in range(shots):
        copies[shot].wait()
        for chan in range(chans):
            shift = shifts[shot, chan]
            part = shift & (LANES - 1)
            base = (chan // 8) * (rows * 8) + chan % 8 + ((shift >> 7) << 3)
            first = held[shot, pl.ds(base, rows, stride=8), :]
            second = held[shot, pl.ds(base + 8, rows, stride=8), :]
            mixed = jnp.where(lane >= part, first, second)
            moved = pltpu.roll(mixed, (LANES - part) & (LANES - 1), 1)
            moved = jnp.where(sample < rows * LANES - shift, moved, 0.0)
            if chan < HALO:
                down_ref[shot, chan] = moved
            if chan >= chans - HALO:
                up_ref[shot, chan - (chans - HALO)] = moved


def align(traces, shifts):
    shots, chans, length = traces.shape
    rows = length // LANES
    flat = traces.reshape(shots, chans // 8, 8, rows, LANES).transpose(0, 1, 3, 2, 4).reshape(-1, LANES)
    edge = jax.ShapeDtypeStruct((shots, HALO, rows, LANES), jnp.float32)
    return pl.pallas_call(
        functools.partial(align_kernel, (shots, chans, rows)),
        out_shape=(edge, edge),
        in_specs=[whole(pltpu.HBM), whole(pltpu.HBM)],
        out_specs=(whole(), whole()),
        scratch_shapes=[
            pltpu.VMEM((shots, chans * rows + TAIL, LANES), jnp.float32),
            pltpu.SMEM((shots, chans), jnp.int32),
            pltpu.SemaphoreType.DMA,
            pltpu.SemaphoreType.DMA((shots,)),
        ],
        compiler_params=pltpu.CompilerParams(vmem_limit_bytes=GRANT),
        name="align",
    )(pltpu.with_memory_space_constraint(shifts, pltpu.HBM), pltpu.with_memory_space_constraint(flat, pltpu.HBM))


def order(a, b):
    return jnp.minimum(a, b), jnp.maximum(a, b)


def medians(values, count):
    total = len(values)
    pairs = {}
    blocks = {}

    def pair(start):
        if start not in pairs:
            pairs[start] = order(values[start], values[start + 1])
        return pairs[start]

    def block(start):
        if start not in blocks:
            (a, b), (c, d) = pair(start), pair(start + 2)
            low, m = order(a, c)
            n, high = order(b, d)
            m, n = order(m, n)
            blocks[start] = (low, m, n, high)
        return blocks[start]

    result = []
    for group in range(-1, (count + 3) // 4):
        wanted = [w for w in range(4 * group + 1, 4 * group + 5) if 0 <= w < count]
        if not wanted:
            continue
        a1, a2, a3, a4 = block(4 * group + 4)
        b1, b2, b3, b4 = block(4 * group + 8)
        t, u = jnp.maximum(a1, b1), jnp.minimum(a3, b3)
        c4 = jnp.maximum(a3, b3)
        c2, c3 = order(t, u)
        d1 = jnp.minimum(a2, b2)
        t, u = jnp.maximum(a2, b2), jnp.minimum(a4, b4)
        d2, d3 = order(t, u)
        m3, (m4, m5), m6 = jnp.maximum(d1, c2), order(d2, c3), jnp.minimum(d3, c4)
        for half, extra in ((0, 4 * group + 2), (1, 4 * group + 12)):
            mine = [w for w in wanted if (w - 4 * group - 1) // 2 == half]
            if not mine:
                continue
            p, q = pair(extra)
            s5 = jnp.minimum(m5, jnp.minimum(jnp.maximum(m4, p), jnp.maximum(m3, q)))
            s6 = jnp.minimum(m6, jnp.minimum(jnp.maximum(m5, p), jnp.maximum(m4, q)))
            for w in mine:
                lone = extra - 1 if (w - 4 * group - 1) == 0 else extra + 2 if (w - 4 * group - 1) == 3 else (
                    4 * group + 12 if half == 0 else 4 * group + 3
                )
                assert w <= lone <= w + 10 and lone < total
                result.append(jnp.maximum(s5, jnp.minimum(s6, values[lone])))
    assert len(result) == count
    return result


def clean_kernel(dims, shifts_ref, low_ref, high_ref, left_ref, down_ref, up_ref, right_ref, out_ref, held):
    shots, chans, rows = dims
    first_shot = lax.axis_index("shot") * shots
    lead = 8
    for chan in range(chans):
        held[chan, pl.ds(0, lead), :] = jnp.zeros((lead, LANES), jnp.float32)
    lane = lax.broadcasted_iota(jnp.int32, (rows, LANES), 1)

    def one_shot(shot, carry):
        def one_part(part, inner):
            place = pl.ds(pl.multiple_of(part * 8, 8), 8)
            values = [left_ref[shot, i, place, :] for i in range(HALO)]
            values += [down_ref[shot, i, place, :] for i in range(HALO)]
            values += [up_ref[shot, i, place, :] for i in range(2 * HALO - chans, HALO)]
            values += [right_ref[shot, i, place, :] for i in range(HALO)]
            once = medians(values, chans + HALO)
            once = [values[HALF + i] - once[i] for i in range(chans + HALO)]
            twice = medians(once, chans)
            stored = pl.ds(pl.multiple_of(lead + part * 8, 8), 8)
            for i in range(chans):
                held[i, stored, :] = once[HALF + i] - twice[i]
            return inner

        lax.fori_loop(0, rows // 8, one_part, 0)
        for chan in range(chans):
            shift = shifts_ref[shot, chan]
            whole_rows, part = shift >> 7, shift & (LANES - 1)
            inside = (first_shot + shot >= low_ref[chan]) & (first_shot + shot < high_ref[chan])
            first = held[chan, pl.ds(lead - whole_rows, rows), :]
            second = held[chan, pl.ds(lead - 1 - whole_rows, rows), :]
            mixed = jnp.where(lane < LANES - part, first, second)
            moved = pltpu.roll(mixed, part, 1)
            out_ref[chan // 2, shot, chan % 2] = jnp.where(inside, moved, 0.0)
        return carry

    lax.fori_loop(0, shots, one_shot, 0)


def clean(shifts, low, high, left, down, up, right, chans, groups):
    shots, _, rows, _ = down.shape
    return pl.pallas_call(
        functools.partial(clean_kernel, (shots, chans, rows)),
        out_shape=jax.ShapeDtypeStruct((groups, shots, chans // groups, rows, LANES), jnp.float32),
        in_specs=[whole(pltpu.SMEM)] * 3 + [whole()] * 4,
        out_specs=whole(),
        scratch_shapes=[pltpu.VMEM((chans, 8 + rows, LANES), jnp.float32)],
        compiler_params=pltpu.CompilerParams(vmem_limit_bytes=GRANT),
        name="clean",
    )(shifts, low, high, left, down, up, right)


def real_forward(x):
    n = len(x)
    if n == 1:
        return [(x[0], None)]
    if n == 2:
        return [(x[0] + x[1], None), (x[0] - x[1], None)]
    even, odd = real_forward(x[0::2]), real_forward(x[1::2])
    out = [None] * (n // 2 + 1)
    for k in range(n // 4 + 1):
        (er, ei), (or_, oi) = even[k], odd[k]
        if k == 0:
            out[0] = (er + or_, None)
            out[n // 2] = (er - or_, None)
        elif 4 * k == n:
            out[k] = (er, -or_)
        else:
            c, s = math_cos(k, n), math_sin(k, n)
            tr, ti = or_ * c + oi * s, oi * c - or_ * s
            out[k] = (er + tr, ei + ti)
            out[n // 2 - k] = (er - tr, ti - ei)
    return out


def real_backward(spectrum, n):
    if n == 1:
        return [spectrum[0][0]]
    if n == 2:
        return [spectrum[0][0] + spectrum[1][0], spectrum[0][0] - spectrum[1][0]]
    even, odd = [None] * (n // 4 + 1), [None] * (n // 4 + 1)
    for k in range(n // 4 + 1):
        (ar, ai), (br, bi) = spectrum[k], spectrum[n // 2 - k]
        if k == 0:
            even[0], odd[0] = (ar + br, None), (ar - br, None)
        elif 4 * k == n:
            even[k], odd[k] = (ar + ar, None), (-(ai + ai), None)
        else:
            c, s = math_cos(k, n), math_sin(k, n)
            even[k] = (ar + br, ai - bi)
            dr, di = ar - br, ai + bi
            odd[k] = (dr * c - di * s, di * c + dr * s)
    first, second = real_backward(even, n // 2), real_backward(odd, n // 2)
    return [v for both in zip(first, second) for v in both]


def math_cos(k, n):
    return float(np.float32(np.cos(2 * np.pi * k / n)))


def math_sin(k, n):
    return float(np.float32(np.sin(2 * np.pi * k / n)))


def split(x):
    top = x.astype(jnp.bfloat16)
    return top, (x - top.astype(jnp.float32)).astype(jnp.bfloat16)


def constant_split(x):
    x = np.asarray(x, np.float32)
    top = x.astype(jnp.bfloat16)
    return top, (x - top.astype(np.float32)).astype(jnp.bfloat16)


def tables(shots, rows):
    a = np.arange(rows)
    outer = 2 * np.pi * (np.outer(a, a) % rows) / rows
    b = np.arange(LANES)
    inner = 2 * np.pi * (np.outer(b, b) % LANES) / LANES
    turn = 2 * np.pi * np.outer(a, b) / (rows * LANES)
    c, s = np.cos(outer), np.sin(outer)
    outer_forward = np.block([[c, s], [-s, c]])
    outer_backward = np.block([[c, -s], [s, c]])
    c, s = np.cos(inner), np.sin(inner)
    inner_forward = np.block([[c, -s], [s, c]])
    inner_backward = np.block([[c, s], [-s, c]]) / (shots * rows * LANES)
    left = []
    for matrix in (outer_forward, outer_backward):
        top, rest = constant_split(matrix)
        left.append(jnp.asarray(np.concatenate([top, top, rest], axis=1)))
    right = []
    for matrix in (inner_forward, inner_backward):
        top, rest = constant_split(matrix)
        right.append(jnp.asarray(np.concatenate([top, top, rest], axis=0)))
    twist = jnp.asarray(np.stack([np.cos(turn), np.sin(turn)]), jnp.float32)
    return (*left, *right, twist)


def dot(a, b):
    return jnp.dot(a, b, preferred_element_type=jnp.float32)


def dip_kernel(dims, bands_ref, data_ref, outer_f, outer_b, inner_f, inner_b, twist_ref, result_ref, held, out_ref, bands, band_sem, sems):
    shots, recs, rows = dims
    high = shots // 2
    band_copy = pltpu.make_async_copy(bands_ref, bands, band_sem)
    band_copy.start()
    first_rec = lax.axis_index("shot") * recs
    lane = lax.broadcasted_iota(jnp.int32, (rows, LANES), 1)
    frequency = lax.broadcasted_iota(jnp.int32, (rows, LANES), 0) + rows * lane
    distance = jnp.minimum(frequency, rows * LANES - frequency)

    for part in range(rows // 8):
        place, below = pl.ds(part * 8, 8), pl.ds(rows + part * 8, 8)
        for rec in range(recs):
            lanes = pl.ds(rec * LANES, LANES)
            out = real_forward([data_ref[shot, rec, place, :] for shot in range(shots)])
            for k in range(high + 1):
                re, im = out[k]
                held[k, place, lanes] = re
                if k > 0:
                    held[k, below, lanes] = jnp.zeros_like(re) if im is None else im

    def left_product(matrix, k):
        top, rest = split(held[k])
        return dot(matrix[...], jnp.concatenate([top, rest, top], axis=0))

    def right_product(lines, matrix):
        top, rest = split(lines)
        return dot(jnp.concatenate([top, rest, top], axis=1), matrix[...])

    def some_waves(step, carry):
        cos, sin = twist_ref[0], twist_ref[1]
        first = 1 + step * WAVES
        lines = []
        for i in range(WAVES):
            spec = left_product(outer_f, first + i)
            for rec in range(recs):
                mine = slice(rec * LANES, (rec + 1) * LANES)
                re, im = spec[:rows, mine], spec[rows:, mine]
                lines.append(jnp.concatenate([re * cos + im * sin, im * cos - re * sin], axis=1))
        wave = right_product(jnp.concatenate(lines, axis=0), inner_f)
        kept = []
        for i in range(WAVES):
            for rec in range(recs):
                n = (i * recs + rec) * rows
                keep = distance >= (first + i) * bands[first_rec + rec]
                kept.append(
                    jnp.concatenate(
                        [
                            jnp.where(keep, wave[n : n + rows, :LANES], 0.0),
                            jnp.where(keep, wave[n : n + rows, LANES:], 0.0),
                        ],
                        axis=1,
                    )
                )
        wave = right_product(jnp.concatenate(kept, axis=0), inner_b)
        for i in range(WAVES):
            for rec in range(recs):
                n = (i * recs + rec) * rows
                lanes = slice(rec * LANES, (rec + 1) * LANES)
                re, im = wave[n : n + rows, :LANES], wave[n : n + rows, LANES:]
                held[first + i, :rows, lanes] = re * cos - im * sin
                held[first + i, rows:, lanes] = im * cos + re * sin
        for i in range(WAVES):
            held[first + i] = left_product(outer_b, first + i)
        return carry

    band_copy.wait()
    lax.fori_loop(0, high // WAVES, some_waves, 0)

    copies = []
    for part in range(rows // 8):
        place, below = pl.ds(part * 8, 8), pl.ds(rows + part * 8, 8)
        for rec in range(recs):
            lanes = pl.ds(rec * LANES, LANES)
            spectrum = [(held[0, place, lanes] * (1.0 / shots), None)]
            for k in range(1, high + 1):
                spectrum.append((held[k, place, lanes], held[k, below, lanes] if k < high else None))
            back = real_backward(spectrum, shots)
            for shot in range(shots):
                out_ref[shot, pl.ds(part * (8 * recs) + rec, 8, stride=recs), :] = back[shot]
        done = pl.ds(part * (8 * recs), 8 * recs)
        copies.append(pltpu.make_async_copy(out_ref.at[:, done], result_ref.at[:, done], sems.at[part]))
        copies[-1].start()
    for copy in copies:
        copy.wait()


def dip_filter(gathered, dip_band):
    shots, recs, rows, _ = gathered.shape
    out = pl.pallas_call(
        functools.partial(dip_kernel, (shots, recs, rows)),
        out_shape=jax.ShapeDtypeStruct((shots, rows * recs, LANES), jnp.float32),
        in_specs=[whole(pltpu.HBM)] + [whole()] * 6,
        out_specs=whole(pltpu.HBM),
        scratch_shapes=[
            pltpu.VMEM((shots // 2 + 1, 2 * rows, recs * LANES), jnp.float32),
            pltpu.VMEM((shots, rows * recs, LANES), jnp.float32),
            pltpu.SMEM(dip_band.shape, jnp.int32),
            pltpu.SemaphoreType.DMA,
            pltpu.SemaphoreType.DMA((rows // 8,)),
        ],
        compiler_params=pltpu.CompilerParams(vmem_limit_bytes=GRANT),
        name="dip",
    )(pltpu.with_memory_space_constraint(dip_band, pltpu.HBM), gathered, *tables(shots, rows))
    return out.reshape(shots, rows, recs, LANES).transpose(0, 2, 1, 3).reshape(shots, recs, rows * LANES)


def local(traces, shifts, aperture_lo, aperture_hi, dip_band):
    shots, chans, length = traces.shape
    blocks, groups = lax.axis_size("chan"), lax.axis_size("shot")
    down, up = align(traces, shifts)
    left = lax.ppermute(up, "chan", [(i, i + 1) for i in range(blocks - 1)])
    right = lax.ppermute(down, "chan", [(i + 1, i) for i in range(blocks - 1)])
    parted = clean(shifts, aperture_lo, aperture_hi, left, down, up, right, chans, groups)
    arrived = lax.all_to_all(parted, "shot", split_axis=0, concat_axis=0, tiled=True)
    gathered = arrived.reshape(groups * shots, chans // groups, length // LANES, LANES)
    return dip_filter(gathered, dip_band)


def solution(mesh):
    return jax.shard_map(
        local,
        mesh=mesh,
        in_specs=(P("shot", "chan", None), P("shot", "chan"), P("chan"), P("chan"), P("chan")),
        out_specs=P(None, ("chan", "shot"), None),
        check_vma=False,
    )
```

```python
import functools

import jax
import jax.numpy as jnp
import numpy as np
from jax import lax
from jax.experimental import pallas as pl
from jax.experimental.pallas import tpu as pltpu
from jax.sharding import PartitionSpec as P


PIECES = (1, 3)
LANES = 128
HALF = 5
HALO = 2 * HALF
TAIL = 8 * 9
GRANT = 16 << 20
WAVES = 16


def whole(space=pltpu.VMEM):
    return pl.BlockSpec(memory_space=space)


def align_kernel(dims, pieces, shifts_ref, traces_ref, *refs):
    edges, (held, shifts, shift_sem, sems) = refs[: 2 * len(pieces)], refs[2 * len(pieces) :]
    shots, chans, rows = dims
    homes = [(piece, shot) for piece, count in enumerate(pieces) for shot in range(count)]
    tiles = chans * rows
    count = pltpu.make_async_copy(shifts_ref, shifts, shift_sem)
    count.start()
    copies = []
    for shot in range(shots):
        source, target = traces_ref.at[pl.ds(shot * tiles, tiles)], held.at[shot, pl.ds(0, tiles)]
        copies.append(pltpu.make_async_copy(source, target, sems.at[shot]))
        copies[-1].start()
        held[shot, pl.ds(tiles, TAIL), :] = jnp.zeros((TAIL, LANES), jnp.float32)
    lane = lax.broadcasted_iota(jnp.int32, (rows, LANES), 1)
    sample = lax.broadcasted_iota(jnp.int32, (rows, LANES), 0) * LANES + lane
    count.wait()
    for shot in range(shots):
        copies[shot].wait()
        piece, slot = homes[shot]
        down_ref, up_ref = edges[2 * piece : 2 * piece + 2]
        for chan in range(chans):
            shift = shifts[shot, chan]
            part = shift & (LANES - 1)
            base = (chan // 8) * (rows * 8) + chan % 8 + ((shift >> 7) << 3)
            first = held[shot, pl.ds(base, rows, stride=8), :]
            second = held[shot, pl.ds(base + 8, rows, stride=8), :]
            mixed = jnp.where(lane >= part, first, second)
            moved = pltpu.roll(mixed, (LANES - part) & (LANES - 1), 1)
            moved = jnp.where(sample < rows * LANES - shift, moved, 0.0)
            if chan < HALO:
                down_ref[slot, chan] = moved
            if chan >= chans - HALO:
                up_ref[slot, chan - (chans - HALO)] = moved


def align(traces, shifts, pieces):
    shots, chans, length = traces.shape
    rows = length // LANES
    flat = traces.reshape(shots, chans // 8, 8, rows, LANES).transpose(0, 1, 3, 2, 4).reshape(-1, LANES)
    edges = [jax.ShapeDtypeStruct((count, HALO, rows, LANES), jnp.float32) for count in pieces for _ in range(2)]
    return pl.pallas_call(
        functools.partial(align_kernel, (shots, chans, rows), pieces),
        out_shape=tuple(edges),
        in_specs=[whole(pltpu.HBM), whole(pltpu.HBM)],
        out_specs=(whole(),) * len(edges),
        scratch_shapes=[
            pltpu.VMEM((shots, chans * rows + TAIL, LANES), jnp.float32),
            pltpu.SMEM((shots, chans), jnp.int32),
            pltpu.SemaphoreType.DMA,
            pltpu.SemaphoreType.DMA((shots,)),
        ],
        compiler_params=pltpu.CompilerParams(vmem_limit_bytes=GRANT),
        name="align",
    )(pltpu.with_memory_space_constraint(shifts, pltpu.HBM), pltpu.with_memory_space_constraint(flat, pltpu.HBM))


def order(a, b):
    return jnp.minimum(a, b), jnp.maximum(a, b)


def medians(values, count):
    total = len(values)
    pairs = {}
    blocks = {}

    def pair(start):
        if start not in pairs:
            pairs[start] = order(values[start], values[start + 1])
        return pairs[start]

    def block(start):
        if start not in blocks:
            (a, b), (c, d) = pair(start), pair(start + 2)
            low, m = order(a, c)
            n, high = order(b, d)
            m, n = order(m, n)
            blocks[start] = (low, m, n, high)
        return blocks[start]

    result = []
    for group in range(-1, (count + 3) // 4):
        wanted = [w for w in range(4 * group + 1, 4 * group + 5) if 0 <= w < count]
        if not wanted:
            continue
        a1, a2, a3, a4 = block(4 * group + 4)
        b1, b2, b3, b4 = block(4 * group + 8)
        t, u = jnp.maximum(a1, b1), jnp.minimum(a3, b3)
        c4 = jnp.maximum(a3, b3)
        c2, c3 = order(t, u)
        d1 = jnp.minimum(a2, b2)
        t, u = jnp.maximum(a2, b2), jnp.minimum(a4, b4)
        d2, d3 = order(t, u)
        m3, (m4, m5), m6 = jnp.maximum(d1, c2), order(d2, c3), jnp.minimum(d3, c4)
        for half, extra in ((0, 4 * group + 2), (1, 4 * group + 12)):
            mine = [w for w in wanted if (w - 4 * group - 1) // 2 == half]
            if not mine:
                continue
            p, q = pair(extra)
            s5 = jnp.minimum(m5, jnp.minimum(jnp.maximum(m4, p), jnp.maximum(m3, q)))
            s6 = jnp.minimum(m6, jnp.minimum(jnp.maximum(m5, p), jnp.maximum(m4, q)))
            for w in mine:
                lone = extra - 1 if (w - 4 * group - 1) == 0 else extra + 2 if (w - 4 * group - 1) == 3 else (
                    4 * group + 12 if half == 0 else 4 * group + 3
                )
                assert w <= lone <= w + 10 and lone < total
                result.append(jnp.maximum(s5, jnp.minimum(s6, values[lone])))
    assert len(result) == count
    return result


def clean_kernel(dims, start, shots_here, shifts_ref, low_ref, high_ref, left_ref, down_ref, up_ref, right_ref, out_ref, held):
    shots, chans, rows = dims
    first_shot = lax.axis_index("shot") * shots_here + start
    lead = 8
    for chan in range(chans):
        held[chan, pl.ds(0, lead), :] = jnp.zeros((lead, LANES), jnp.float32)
    lane = lax.broadcasted_iota(jnp.int32, (rows, LANES), 1)

    def one_shot(shot, carry):
        def one_part(part, inner):
            place = pl.ds(pl.multiple_of(part * 8, 8), 8)
            values = [left_ref[shot, i, place, :] for i in range(HALO)]
            values += [down_ref[shot, i, place, :] for i in range(HALO)]
            values += [up_ref[shot, i, place, :] for i in range(2 * HALO - chans, HALO)]
            values += [right_ref[shot, i, place, :] for i in range(HALO)]
            once = medians(values, chans + HALO)
            once = [values[HALF + i] - once[i] for i in range(chans + HALO)]
            twice = medians(once, chans)
            stored = pl.ds(pl.multiple_of(lead + part * 8, 8), 8)
            for i in range(chans):
                held[i, stored, :] = once[HALF + i] - twice[i]
            return inner

        lax.fori_loop(0, rows // 8, one_part, 0)
        for chan in range(chans):
            shift = shifts_ref[start + shot, chan]
            whole_rows, part = shift >> 7, shift & (LANES - 1)
            inside = (first_shot + shot >= low_ref[chan]) & (first_shot + shot < high_ref[chan])
            first = held[chan, pl.ds(lead - whole_rows, rows), :]
            second = held[chan, pl.ds(lead - 1 - whole_rows, rows), :]
            mixed = jnp.where(lane < LANES - part, first, second)
            moved = pltpu.roll(mixed, part, 1)
            out_ref[chan // 2, shot, chan % 2] = jnp.where(inside, moved, 0.0)
        return carry

    lax.fori_loop(0, shots, one_shot, 0)


def clean(shifts, low, high, left, down, up, right, start, groups):
    shots, _, rows, _ = down.shape
    shots_here, chans = shifts.shape
    return pl.pallas_call(
        functools.partial(clean_kernel, (shots, chans, rows), start, shots_here),
        out_shape=jax.ShapeDtypeStruct((groups, shots, chans // groups, rows, LANES), jnp.float32),
        in_specs=[whole(pltpu.SMEM)] * 3 + [whole()] * 4,
        out_specs=whole(),
        scratch_shapes=[pltpu.VMEM((chans, 8 + rows, LANES), jnp.float32)],
        compiler_params=pltpu.CompilerParams(vmem_limit_bytes=GRANT),
        name="clean",
    )(shifts, low, high, left, down, up, right)


def real_forward(x):
    n = len(x)
    if n == 1:
        return [(x[0], None)]
    if n == 2:
        return [(x[0] + x[1], None), (x[0] - x[1], None)]
    even, odd = real_forward(x[0::2]), real_forward(x[1::2])
    out = [None] * (n // 2 + 1)
    for k in range(n // 4 + 1):
        (er, ei), (or_, oi) = even[k], odd[k]
        if k == 0:
            out[0] = (er + or_, None)
            out[n // 2] = (er - or_, None)
        elif 4 * k == n:
            out[k] = (er, -or_)
        else:
            c, s = math_cos(k, n), math_sin(k, n)
            tr, ti = or_ * c + oi * s, oi * c - or_ * s
            out[k] = (er + tr, ei + ti)
            out[n // 2 - k] = (er - tr, ti - ei)
    return out


def real_backward(spectrum, n):
    if n == 1:
        return [spectrum[0][0]]
    if n == 2:
        return [spectrum[0][0] + spectrum[1][0], spectrum[0][0] - spectrum[1][0]]
    even, odd = [None] * (n // 4 + 1), [None] * (n // 4 + 1)
    for k in range(n // 4 + 1):
        (ar, ai), (br, bi) = spectrum[k], spectrum[n // 2 - k]
        if k == 0:
            even[0], odd[0] = (ar + br, None), (ar - br, None)
        elif 4 * k == n:
            even[k], odd[k] = (ar + ar, None), (-(ai + ai), None)
        else:
            c, s = math_cos(k, n), math_sin(k, n)
            even[k] = (ar + br, ai - bi)
            dr, di = ar - br, ai + bi
            odd[k] = (dr * c - di * s, di * c + dr * s)
    first, second = real_backward(even, n // 2), real_backward(odd, n // 2)
    return [v for both in zip(first, second) for v in both]


def math_cos(k, n):
    return float(np.float32(np.cos(2 * np.pi * k / n)))


def math_sin(k, n):
    return float(np.float32(np.sin(2 * np.pi * k / n)))


def split(x):
    top = x.astype(jnp.bfloat16)
    return top, (x - top.astype(jnp.float32)).astype(jnp.bfloat16)


def constant_split(x):
    x = np.asarray(x, np.float32)
    top = x.astype(jnp.bfloat16)
    return top, (x - top.astype(np.float32)).astype(jnp.bfloat16)


def tables(shots, rows):
    a = np.arange(rows)
    outer = 2 * np.pi * (np.outer(a, a) % rows) / rows
    b = np.arange(LANES)
    inner = 2 * np.pi * (np.outer(b, b) % LANES) / LANES
    turn = 2 * np.pi * np.outer(a, b) / (rows * LANES)
    c, s = np.cos(outer), np.sin(outer)
    outer_forward = np.block([[c, s], [-s, c]])
    outer_backward = np.block([[c, -s], [s, c]])
    c, s = np.cos(inner), np.sin(inner)
    inner_forward = np.block([[c, -s], [s, c]])
    inner_backward = np.block([[c, s], [-s, c]]) / (shots * rows * LANES)
    left = []
    for matrix in (outer_forward, outer_backward):
        top, rest = constant_split(matrix)
        left.append(jnp.asarray(np.concatenate([top, top, rest], axis=1)))
    right = []
    for matrix in (inner_forward, inner_backward):
        top, rest = constant_split(matrix)
        right.append(jnp.asarray(np.concatenate([top, top, rest], axis=0)))
    twist = jnp.asarray(np.stack([np.cos(turn), np.sin(turn)]), jnp.float32)
    return (*left, *right, twist)


def dot(a, b):
    return jnp.dot(a, b, preferred_element_type=jnp.float32)


def dip_kernel(dims, pieces, bands_ref, *refs):
    data_refs, refs = refs[: len(pieces)], refs[len(pieces) :]
    outer_f, outer_b, inner_f, inner_b, twist_ref, result_ref, held, out_ref, bands, band_sem, sems = refs
    shots, recs, rows = dims
    high = shots // 2
    band_copy = pltpu.make_async_copy(bands_ref, bands, band_sem)
    band_copy.start()
    first_rec = lax.axis_index("shot") * recs
    lane = lax.broadcasted_iota(jnp.int32, (rows, LANES), 1)
    frequency = lax.broadcasted_iota(jnp.int32, (rows, LANES), 0) + rows * lane
    distance = jnp.minimum(frequency, rows * LANES - frequency)

    for part in range(rows // 8):
        place, below = pl.ds(part * 8, 8), pl.ds(rows + part * 8, 8)
        for rec in range(recs):
            lanes = pl.ds(rec * LANES, LANES)
            gathered = [
                data_refs[piece][group, slot, rec, place, :]
                for group in range(shots // sum(pieces))
                for piece, count in enumerate(pieces)
                for slot in range(count)
            ]
            out = real_forward(gathered)
            for k in range(high + 1):
                re, im = out[k]
                held[k, place, lanes] = re
                if k > 0:
                    held[k, below, lanes] = jnp.zeros_like(re) if im is None else im

    def left_product(matrix, k):
        top, rest = split(held[k])
        return dot(matrix[...], jnp.concatenate([top, rest, top], axis=0))

    def right_product(lines, matrix):
        top, rest = split(lines)
        return dot(jnp.concatenate([top, rest, top], axis=1), matrix[...])

    def some_waves(step, carry):
        cos, sin = twist_ref[0], twist_ref[1]
        first = 1 + step * WAVES
        lines = []
        for i in range(WAVES):
            spec = left_product(outer_f, first + i)
            for rec in range(recs):
                mine = slice(rec * LANES, (rec + 1) * LANES)
                re, im = spec[:rows, mine], spec[rows:, mine]
                lines.append(jnp.concatenate([re * cos + im * sin, im * cos - re * sin], axis=1))
        wave = right_product(jnp.concatenate(lines, axis=0), inner_f)
        kept = []
        for i in range(WAVES):
            for rec in range(recs):
                n = (i * recs + rec) * rows
                keep = distance >= (first + i) * bands[first_rec + rec]
                kept.append(
                    jnp.concatenate(
                        [
                            jnp.where(keep, wave[n : n + rows, :LANES], 0.0),
                            jnp.where(keep, wave[n : n + rows, LANES:], 0.0),
                        ],
                        axis=1,
                    )
                )
        wave = right_product(jnp.concatenate(kept, axis=0), inner_b)
        for i in range(WAVES):
            for rec in range(recs):
                n = (i * recs + rec) * rows
                lanes = slice(rec * LANES, (rec + 1) * LANES)
                re, im = wave[n : n + rows, :LANES], wave[n : n + rows, LANES:]
                held[first + i, :rows, lanes] = re * cos - im * sin
                held[first + i, rows:, lanes] = im * cos + re * sin
        for i in range(WAVES):
            held[first + i] = left_product(outer_b, first + i)
        return carry

    band_copy.wait()
    lax.fori_loop(0, high // WAVES, some_waves, 0)

    copies = []
    for part in range(rows // 8):
        place, below = pl.ds(part * 8, 8), pl.ds(rows + part * 8, 8)
        for rec in range(recs):
            lanes = pl.ds(rec * LANES, LANES)
            spectrum = [(held[0, place, lanes] * (1.0 / shots), None)]
            for k in range(1, high + 1):
                spectrum.append((held[k, place, lanes], held[k, below, lanes] if k < high else None))
            back = real_backward(spectrum, shots)
            for shot in range(shots):
                out_ref[shot, pl.ds(part * (8 * recs) + rec, 8, stride=recs), :] = back[shot]
        done = pl.ds(part * (8 * recs), 8 * recs)
        copies.append(pltpu.make_async_copy(out_ref.at[:, done], result_ref.at[:, done], sems.at[part]))
        copies[-1].start()
    for copy in copies:
        copy.wait()


def dip_filter(gathered, dip_band):
    groups, _, recs, rows, _ = gathered[0].shape
    pieces = tuple(piece.shape[1] for piece in gathered)
    shots = groups * sum(pieces)
    out = pl.pallas_call(
        functools.partial(dip_kernel, (shots, recs, rows), pieces),
        out_shape=jax.ShapeDtypeStruct((shots, rows * recs, LANES), jnp.float32),
        in_specs=[whole(pltpu.HBM)] + [whole()] * (5 + len(gathered)),
        out_specs=whole(pltpu.HBM),
        scratch_shapes=[
            pltpu.VMEM((shots // 2 + 1, 2 * rows, recs * LANES), jnp.float32),
            pltpu.VMEM((shots, rows * recs, LANES), jnp.float32),
            pltpu.SMEM(dip_band.shape, jnp.int32),
            pltpu.SemaphoreType.DMA,
            pltpu.SemaphoreType.DMA((rows // 8,)),
        ],
        compiler_params=pltpu.CompilerParams(vmem_limit_bytes=GRANT),
        name="dip",
    )(pltpu.with_memory_space_constraint(dip_band, pltpu.HBM), *gathered, *tables(shots, rows))
    return out.reshape(shots, rows, recs, LANES).transpose(0, 2, 1, 3).reshape(shots, recs, rows * LANES)


def local(traces, shifts, aperture_lo, aperture_hi, dip_band):
    blocks, groups = lax.axis_size("chan"), lax.axis_size("shot")
    upward, downward = [(i, i + 1) for i in range(blocks - 1)], [(i + 1, i) for i in range(blocks - 1)]
    edges = align(traces, shifts, PIECES)
    sides = []
    for i in range(len(PIECES)):
        down, up = edges[2 * i : 2 * i + 2]
        left = lax.ppermute(up, "chan", upward)
        right = lax.ppermute(down, "chan", downward)
        sides.append((left, down, up, right))
    arrived = []
    for i in range(len(PIECES)):
        parted = clean(shifts, aperture_lo, aperture_hi, *sides[i], sum(PIECES[:i]), groups)
        arrived.append(lax.all_to_all(parted, "shot", split_axis=0, concat_axis=0, tiled=True))
    return dip_filter(arrived, dip_band)


def solution(mesh):
    return jax.shard_map(
        local,
        mesh=mesh,
        in_specs=(P("shot", "chan", None), P("shot", "chan"), P("chan"), P("chan"), P("chan")),
        out_specs=P(None, ("chan", "shot"), None),
        check_vma=False,
    )
```

```python
import functools

import jax
import jax.numpy as jnp
import numpy as np
from jax import lax
from jax.experimental import pallas as pl
from jax.experimental.pallas import tpu as pltpu
from jax.sharding import PartitionSpec as P


PIECES = (1, 3)
LANES = 128
HALF = 5
HALO = 2 * HALF
TAIL = 8 * 9
GRANT = 16 << 20
PARTS = 2
WAVES = 16


def whole(space=pltpu.VMEM):
    return pl.BlockSpec(memory_space=space)


def align_kernel(dims, pieces, shifts_ref, traces_ref, *refs):
    edges, (held, shifts, shift_sem, sems) = refs[: 2 * len(pieces)], refs[2 * len(pieces) :]
    shots, chans, rows = dims
    homes = [(piece, shot) for piece, count in enumerate(pieces) for shot in range(count)]
    tiles = chans * rows
    count = pltpu.make_async_copy(shifts_ref, shifts, shift_sem)
    count.start()
    copies = []
    for shot in range(shots):
        source, target = traces_ref.at[pl.ds(shot * tiles, tiles)], held.at[shot, pl.ds(0, tiles)]
        copies.append(pltpu.make_async_copy(source, target, sems.at[shot]))
        copies[-1].start()
        held[shot, pl.ds(tiles, TAIL), :] = jnp.zeros((TAIL, LANES), jnp.float32)
    lane = lax.broadcasted_iota(jnp.int32, (rows, LANES), 1)
    sample = lax.broadcasted_iota(jnp.int32, (rows, LANES), 0) * LANES + lane
    count.wait()
    for shot in range(shots):
        if shot < 2:
            for copy in copies[shot : 1 + shot * shots]:
                copy.wait()
        piece, slot = homes[shot]
        down_ref, up_ref = edges[2 * piece : 2 * piece + 2]
        for chan in range(chans):
            shift = shifts[shot, chan]
            part = shift & (LANES - 1)
            base = (chan // 8) * (rows * 8) + chan % 8 + ((shift >> 7) << 3)
            first = held[shot, pl.ds(base, rows, stride=8), :]
            second = held[shot, pl.ds(base + 8, rows, stride=8), :]
            mixed = jnp.where(lane >= part, first, second)
            moved = pltpu.roll(mixed, (LANES - part) & (LANES - 1), 1)
            moved = jnp.where(sample < rows * LANES - shift, moved, 0.0)
            if chan < HALO:
                down_ref[slot, chan] = moved
            if chan >= chans - HALO:
                up_ref[slot, chan - (chans - HALO)] = moved


def align(traces, shifts, pieces):
    shots, chans, length = traces.shape
    rows = length // LANES
    flat = traces.reshape(shots, chans // 8, 8, rows, LANES).transpose(0, 1, 3, 2, 4).reshape(-1, LANES)
    edges = [jax.ShapeDtypeStruct((count, HALO, rows, LANES), jnp.float32) for count in pieces for _ in range(2)]
    return pl.pallas_call(
        functools.partial(align_kernel, (shots, chans, rows), pieces),
        out_shape=tuple(edges),
        in_specs=[whole(pltpu.HBM), whole(pltpu.HBM)],
        out_specs=(whole(),) * len(edges),
        scratch_shapes=[
            pltpu.VMEM((shots, chans * rows + TAIL, LANES), jnp.float32),
            pltpu.SMEM((shots, chans), jnp.int32),
            pltpu.SemaphoreType.DMA,
            pltpu.SemaphoreType.DMA((shots,)),
        ],
        compiler_params=pltpu.CompilerParams(vmem_limit_bytes=GRANT),
        name="align",
    )(pltpu.with_memory_space_constraint(shifts, pltpu.HBM), pltpu.with_memory_space_constraint(flat, pltpu.HBM))


def order(a, b):
    return jnp.minimum(a, b), jnp.maximum(a, b)


def medians(values, count):
    total = len(values)
    pairs = {}
    blocks = {}

    def pair(start):
        if start not in pairs:
            pairs[start] = order(values[start], values[start + 1])
        return pairs[start]

    def block(start):
        if start not in blocks:
            (a, b), (c, d) = pair(start), pair(start + 2)
            low, m = order(a, c)
            n, high = order(b, d)
            m, n = order(m, n)
            blocks[start] = (low, m, n, high)
        return blocks[start]

    result = []
    for group in range(-1, (count + 3) // 4):
        wanted = [w for w in range(4 * group + 1, 4 * group + 5) if 0 <= w < count]
        if not wanted:
            continue
        a1, a2, a3, a4 = block(4 * group + 4)
        b1, b2, b3, b4 = block(4 * group + 8)
        t, u = jnp.maximum(a1, b1), jnp.minimum(a3, b3)
        c4 = jnp.maximum(a3, b3)
        c2, c3 = order(t, u)
        d1 = jnp.minimum(a2, b2)
        t, u = jnp.maximum(a2, b2), jnp.minimum(a4, b4)
        d2, d3 = order(t, u)
        m3, (m4, m5), m6 = jnp.maximum(d1, c2), order(d2, c3), jnp.minimum(d3, c4)
        for half, extra in ((0, 4 * group + 2), (1, 4 * group + 12)):
            mine = [w for w in wanted if (w - 4 * group - 1) // 2 == half]
            if not mine:
                continue
            p, q = pair(extra)
            s5 = jnp.minimum(m5, jnp.minimum(jnp.maximum(m4, p), jnp.maximum(m3, q)))
            s6 = jnp.minimum(m6, jnp.minimum(jnp.maximum(m5, p), jnp.maximum(m4, q)))
            for w in mine:
                lone = extra - 1 if (w - 4 * group - 1) == 0 else extra + 2 if (w - 4 * group - 1) == 3 else (
                    4 * group + 12 if half == 0 else 4 * group + 3
                )
                assert w <= lone <= w + 10 and lone < total
                result.append(jnp.maximum(s5, jnp.minimum(s6, values[lone])))
    assert len(result) == count
    return result


def clean_kernel(dims, start, shots_here, shifts_ref, low_ref, high_ref, left_ref, down_ref, up_ref, right_ref, out_ref, held):
    shots, chans, rows = dims
    first_shot = lax.axis_index("shot") * shots_here + start
    lead = 8
    for slot in range(2):
        for chan in range(chans):
            held[slot, chan, pl.ds(0, lead), :] = jnp.zeros((lead, LANES), jnp.float32)
    lane = lax.broadcasted_iota(jnp.int32, (rows, LANES), 1)

    def passes(shot, part):
        place = pl.ds(part * 8, 8)
        values = [left_ref[shot, i, place, :] for i in range(HALO)]
        values += [down_ref[shot, i, place, :] for i in range(HALO)]
        values += [up_ref[shot, i, place, :] for i in range(2 * HALO - chans, HALO)]
        values += [right_ref[shot, i, place, :] for i in range(HALO)]
        once = medians(values, chans + HALO)
        once = [values[HALF + i] - once[i] for i in range(chans + HALO)]
        twice = medians(once, chans)
        for i in range(chans):
            held[shot % 2, i, pl.ds(lead + part * 8, 8), :] = once[HALF + i] - twice[i]

    def restore(shot, chan):
        shift = shifts_ref[start + shot, chan]
        whole_rows, part = shift >> 7, shift & (LANES - 1)
        inside = (first_shot + shot >= low_ref[chan]) & (first_shot + shot < high_ref[chan])
        first = held[shot % 2, chan, pl.ds(lead - whole_rows, rows), :]
        second = held[shot % 2, chan, pl.ds(lead - 1 - whole_rows, rows), :]
        mixed = jnp.where(lane < LANES - part, first, second)
        moved = pltpu.roll(mixed, part, 1)
        out_ref[chan // 2, shot, chan % 2] = jnp.where(inside, moved, 0.0)

    parts = rows // 8
    for shot in range(shots + 1):
        for part in range(parts):
            if shot < shots:
                passes(shot, part)
            if shot > 0:
                for chan in range(part * chans // parts, (part + 1) * chans // parts):
                    restore(shot - 1, chan)


def clean(shifts, low, high, left, down, up, right, start, groups):
    shots, _, rows, _ = down.shape
    shots_here, chans = shifts.shape
    return pl.pallas_call(
        functools.partial(clean_kernel, (shots, chans, rows), start, shots_here),
        out_shape=jax.ShapeDtypeStruct((groups, shots, chans // groups, rows, LANES), jnp.float32),
        in_specs=[whole(pltpu.SMEM)] * 3 + [whole()] * 4,
        out_specs=whole(),
        scratch_shapes=[pltpu.VMEM((2, chans, 8 + rows, LANES), jnp.float32)],
        compiler_params=pltpu.CompilerParams(vmem_limit_bytes=GRANT),
        name="clean",
    )(shifts, low, high, left, down, up, right)


def real_forward(x):
    n = len(x)
    if n == 1:
        return [(x[0], None)]
    if n == 2:
        return [(x[0] + x[1], None), (x[0] - x[1], None)]
    even, odd = real_forward(x[0::2]), real_forward(x[1::2])
    out = [None] * (n // 2 + 1)
    for k in range(n // 4 + 1):
        (er, ei), (or_, oi) = even[k], odd[k]
        if k == 0:
            out[0] = (er + or_, None)
            out[n // 2] = (er - or_, None)
        elif 4 * k == n:
            out[k] = (er, -or_)
        else:
            c, s = math_cos(k, n), math_sin(k, n)
            tr, ti = or_ * c + oi * s, oi * c - or_ * s
            out[k] = (er + tr, ei + ti)
            out[n // 2 - k] = (er - tr, ti - ei)
    return out


def real_backward(spectrum, n):
    if n == 1:
        return [spectrum[0][0]]
    if n == 2:
        return [spectrum[0][0] + spectrum[1][0], spectrum[0][0] - spectrum[1][0]]
    even, odd = [None] * (n // 4 + 1), [None] * (n // 4 + 1)
    for k in range(n // 4 + 1):
        (ar, ai), (br, bi) = spectrum[k], spectrum[n // 2 - k]
        if k == 0:
            even[0], odd[0] = (ar + br, None), (ar - br, None)
        elif 4 * k == n:
            even[k], odd[k] = (ar + ar, None), (-(ai + ai), None)
        else:
            c, s = math_cos(k, n), math_sin(k, n)
            even[k] = (ar + br, ai - bi)
            dr, di = ar - br, ai + bi
            odd[k] = (dr * c - di * s, di * c + dr * s)
    first, second = real_backward(even, n // 2), real_backward(odd, n // 2)
    return [v for both in zip(first, second) for v in both]


def math_cos(k, n):
    return float(np.float32(np.cos(2 * np.pi * k / n)))


def math_sin(k, n):
    return float(np.float32(np.sin(2 * np.pi * k / n)))


def split(x):
    top = x.astype(jnp.bfloat16)
    return top, (x - top.astype(jnp.float32)).astype(jnp.bfloat16)


def constant_split(x):
    x = np.asarray(x, np.float32)
    top = x.astype(jnp.bfloat16)
    return top, (x - top.astype(np.float32)).astype(jnp.bfloat16)


def tables(shots, rows):
    a = np.arange(rows)
    outer = 2 * np.pi * (np.outer(a, a) % rows) / rows
    b = np.arange(LANES)
    inner = 2 * np.pi * (np.outer(b, b) % LANES) / LANES
    turn = 2 * np.pi * np.outer(a, b) / (rows * LANES)
    c, s = np.cos(outer), np.sin(outer)
    outer_forward = np.block([[c, s], [-s, c]])
    outer_backward = np.block([[c, -s], [s, c]])
    c, s = np.cos(inner), np.sin(inner)
    inner_forward = np.block([[c, -s], [s, c]])
    inner_backward = np.block([[c, s], [-s, c]]) / (shots * rows * LANES)
    left = []
    for matrix in (outer_forward, outer_backward):
        top, rest = constant_split(matrix)
        left.append(jnp.asarray(np.concatenate([top, top, rest], axis=1)))
    right = []
    for matrix in (inner_forward, inner_backward):
        top, rest = constant_split(matrix)
        right.append(jnp.asarray(np.concatenate([top, top, rest], axis=0)))
    twist = jnp.asarray(np.stack([np.cos(turn), np.sin(turn)]), jnp.float32)
    return (*left, *right, twist)


def dot(a, b):
    return jnp.dot(a, b, preferred_element_type=jnp.float32)


def dip_kernel(dims, pieces, bands_ref, *refs):
    data_refs, refs = refs[: len(pieces)], refs[len(pieces) :]
    outer_f, outer_b, inner_f, inner_b, twist_ref, result_ref, held, out_ref, bands, band_sem, sems = refs
    shots, recs, rows = dims
    high = shots // 2
    band_copy = pltpu.make_async_copy(bands_ref, bands, band_sem)
    band_copy.start()
    first_rec = lax.axis_index("shot") * recs
    lane = lax.broadcasted_iota(jnp.int32, (rows, LANES), 1)
    frequency = lax.broadcasted_iota(jnp.int32, (rows, LANES), 0) + rows * lane
    distance = jnp.minimum(frequency, rows * LANES - frequency)

    for part in range(rows // 8):
        place, below = pl.ds(part * 8, 8), pl.ds(rows + part * 8, 8)
        for rec in range(recs):
            lanes = pl.ds(rec * LANES, LANES)
            gathered = [
                data_refs[piece][group, slot, rec, place, :]
                for group in range(shots // sum(pieces))
                for piece, count in enumerate(pieces)
                for slot in range(count)
            ]
            out = real_forward(gathered)
            for k in range(high + 1):
                re, im = out[k]
                held[k, place, lanes] = re
                if k > 0:
                    held[k, below, lanes] = jnp.zeros_like(re) if im is None else im

    def left_product(matrix, k):
        top, rest = split(held[k])
        return dot(matrix[...], jnp.concatenate([top, rest, top], axis=0))

    def right_product(lines, matrix):
        size = len(lines) // PARTS
        done = []
        for i in range(PARTS):
            top, rest = split(jnp.concatenate(lines[i * size : (i + 1) * size], axis=0))
            done.append(dot(jnp.concatenate([top, rest, top], axis=1), matrix[...]))
        return jnp.concatenate(done, axis=0)

    def some_waves(step):
        cos, sin = twist_ref[0], twist_ref[1]
        first = 1 + step * WAVES
        lines = []
        for i in range(WAVES):
            spec = left_product(outer_f, first + i)
            for rec in range(recs):
                mine = slice(rec * LANES, (rec + 1) * LANES)
                re, im = spec[:rows, mine], spec[rows:, mine]
                lines.append(jnp.concatenate([re * cos + im * sin, im * cos - re * sin], axis=1))
        wave = right_product(lines, inner_f)
        kept = []
        for i in range(WAVES):
            for rec in range(recs):
                n = (i * recs + rec) * rows
                keep = distance >= (first + i) * bands[first_rec + rec]
                kept.append(
                    jnp.concatenate(
                        [
                            jnp.where(keep, wave[n : n + rows, :LANES], 0.0),
                            jnp.where(keep, wave[n : n + rows, LANES:], 0.0),
                        ],
                        axis=1,
                    )
                )
        wave = right_product(kept, inner_b)
        for i in range(WAVES):
            for rec in range(recs):
                n = (i * recs + rec) * rows
                lanes = slice(rec * LANES, (rec + 1) * LANES)
                re, im = wave[n : n + rows, :LANES], wave[n : n + rows, LANES:]
                held[first + i, :rows, lanes] = re * cos - im * sin
                held[first + i, rows:, lanes] = im * cos + re * sin
        for i in range(WAVES):
            held[first + i] = left_product(outer_b, first + i)

    band_copy.wait()
    for step in range(high // WAVES):
        some_waves(step)

    copies = []
    for part in range(rows // 8):
        place, below = pl.ds(part * 8, 8), pl.ds(rows + part * 8, 8)
        for rec in range(recs):
            lanes = pl.ds(rec * LANES, LANES)
            spectrum = [(held[0, place, lanes] * (1.0 / shots), None)]
            for k in range(1, high + 1):
                spectrum.append((held[k, place, lanes], held[k, below, lanes] if k < high else None))
            back = real_backward(spectrum, shots)
            for shot in range(shots):
                out_ref[shot, pl.ds(part * (8 * recs) + rec, 8, stride=recs), :] = back[shot]
        done = pl.ds(part * (8 * recs), 8 * recs)
        copies.append(pltpu.make_async_copy(out_ref.at[:, done], result_ref.at[:, done], sems.at[part]))
        copies[-1].start()
    for copy in copies:
        copy.wait()


def dip_filter(gathered, dip_band):
    groups, _, recs, rows, _ = gathered[0].shape
    pieces = tuple(piece.shape[1] for piece in gathered)
    shots = groups * sum(pieces)
    out = pl.pallas_call(
        functools.partial(dip_kernel, (shots, recs, rows), pieces),
        out_shape=jax.ShapeDtypeStruct((shots, rows * recs, LANES), jnp.float32),
        in_specs=[whole(pltpu.HBM)] + [whole()] * (5 + len(gathered)),
        out_specs=whole(pltpu.HBM),
        scratch_shapes=[
            pltpu.VMEM((shots // 2 + 1, 2 * rows, recs * LANES), jnp.float32),
            pltpu.VMEM((shots, rows * recs, LANES), jnp.float32),
            pltpu.SMEM(dip_band.shape, jnp.int32),
            pltpu.SemaphoreType.DMA,
            pltpu.SemaphoreType.DMA((rows // 8,)),
        ],
        compiler_params=pltpu.CompilerParams(vmem_limit_bytes=GRANT),
        name="dip",
    )(pltpu.with_memory_space_constraint(dip_band, pltpu.HBM), *gathered, *tables(shots, rows))
    return out.reshape(shots, rows, recs, LANES).transpose(0, 2, 1, 3).reshape(shots, recs, rows * LANES)


def local(traces, shifts, aperture_lo, aperture_hi, dip_band):
    blocks, groups = lax.axis_size("chan"), lax.axis_size("shot")
    upward, downward = [(i, i + 1) for i in range(blocks - 1)], [(i + 1, i) for i in range(blocks - 1)]
    edges = align(traces, shifts, PIECES)
    sides = []
    for i in range(len(PIECES)):
        down, up = edges[2 * i : 2 * i + 2]
        left = lax.ppermute(up, "chan", upward)
        right = lax.ppermute(down, "chan", downward)
        sides.append((left, down, up, right))
    arrived = []
    for i in range(len(PIECES)):
        parted = clean(shifts, aperture_lo, aperture_hi, *sides[i], sum(PIECES[:i]), groups)
        arrived.append(lax.all_to_all(parted, "shot", split_axis=0, concat_axis=0, tiled=True))
    return dip_filter(arrived, dip_band)


def solution(mesh):
    return jax.shard_map(
        local,
        mesh=mesh,
        in_specs=(P("shot", "chan", None), P("shot", "chan"), P("chan"), P("chan"), P("chan")),
        out_specs=P(None, ("chan", "shot"), None),
        check_vma=False,
    )
```

```python
import functools

import jax
import jax.numpy as jnp
import numpy as np
from jax import lax
from jax.experimental import pallas as pl
from jax.experimental.pallas import tpu as pltpu
from jax.sharding import PartitionSpec as P


PIECES = (1, 3)
LANES = 128
HALF = 5
HALO = 2 * HALF
TAIL = 8 * 9
GRANT = 16 << 20
PARTS = 2
WAVES = 16


def whole(space=pltpu.VMEM):
    return pl.BlockSpec(memory_space=space)


def align_kernel(dims, pieces, shifts_ref, traces_ref, *refs):
    edges, (held, shifts, shift_sem, sems) = refs[: 2 * len(pieces)], refs[2 * len(pieces) :]
    shots, chans, rows = dims
    homes = [(piece, shot) for piece, count in enumerate(pieces) for shot in range(count)]
    tiles = chans * rows
    count = pltpu.make_async_copy(shifts_ref, shifts, shift_sem)
    count.start()
    copies = []
    for shot in range(shots):
        source, target = traces_ref.at[pl.ds(shot * tiles, tiles)], held.at[shot, pl.ds(0, tiles)]
        copies.append(pltpu.make_async_copy(source, target, sems.at[shot]))
        copies[-1].start()
        held[shot, pl.ds(tiles, TAIL), :] = jnp.zeros((TAIL, LANES), jnp.float32)
    lane = lax.broadcasted_iota(jnp.int32, (rows, LANES), 1)
    sample = lax.broadcasted_iota(jnp.int32, (rows, LANES), 0) * LANES + lane
    count.wait()
    for shot in range(shots):
        if shot < 2:
            for copy in copies[shot : 1 + shot * shots]:
                copy.wait()
        piece, slot = homes[shot]
        down_ref, up_ref = edges[2 * piece : 2 * piece + 2]
        for chan in range(chans):
            shift = shifts[shot, chan]
            part = shift & (LANES - 1)
            base = (chan // 8) * (rows * 8) + chan % 8 + ((shift >> 7) << 3)
            first = held[shot, pl.ds(base, rows, stride=8), :]
            second = held[shot, pl.ds(base + 8, rows, stride=8), :]
            mixed = jnp.where(lane >= part, first, second)
            moved = pltpu.roll(mixed, (LANES - part) & (LANES - 1), 1)
            moved = jnp.where(sample < rows * LANES - shift, moved, 0.0)
            if chan < HALO:
                down_ref[slot, chan] = moved
            if chan >= chans - HALO:
                up_ref[slot, chan - (chans - HALO)] = moved


def align(traces, shifts, pieces):
    shots, chans, length = traces.shape
    rows = length // LANES
    flat = traces.reshape(shots, chans // 8, 8, rows, LANES).transpose(0, 1, 3, 2, 4).reshape(-1, LANES)
    edges = [jax.ShapeDtypeStruct((count, HALO, rows, LANES), jnp.float32) for count in pieces for _ in range(2)]
    return pl.pallas_call(
        functools.partial(align_kernel, (shots, chans, rows), pieces),
        out_shape=tuple(edges),
        in_specs=[whole(pltpu.HBM), whole(pltpu.HBM)],
        out_specs=(whole(),) * len(edges),
        scratch_shapes=[
            pltpu.VMEM((shots, chans * rows + TAIL, LANES), jnp.float32),
            pltpu.SMEM((shots, chans), jnp.int32),
            pltpu.SemaphoreType.DMA,
            pltpu.SemaphoreType.DMA((shots,)),
        ],
        compiler_params=pltpu.CompilerParams(vmem_limit_bytes=GRANT),
        name="align",
    )(pltpu.with_memory_space_constraint(shifts, pltpu.HBM), pltpu.with_memory_space_constraint(flat, pltpu.HBM))


def order(a, b):
    return jnp.minimum(a, b), jnp.maximum(a, b)


def medians(values, count):
    total = len(values)
    pairs = {}
    blocks = {}

    def pair(start):
        if start not in pairs:
            pairs[start] = order(values[start], values[start + 1])
        return pairs[start]

    def block(start):
        if start not in blocks:
            (a, b), (c, d) = pair(start), pair(start + 2)
            low, m = order(a, c)
            n, high = order(b, d)
            m, n = order(m, n)
            blocks[start] = (low, m, n, high)
        return blocks[start]

    result = []
    for group in range(-1, (count + 3) // 4):
        wanted = [w for w in range(4 * group + 1, 4 * group + 5) if 0 <= w < count]
        if not wanted:
            continue
        a1, a2, a3, a4 = block(4 * group + 4)
        b1, b2, b3, b4 = block(4 * group + 8)
        t, u = jnp.maximum(a1, b1), jnp.minimum(a3, b3)
        c4 = jnp.maximum(a3, b3)
        c2, c3 = order(t, u)
        d1 = jnp.minimum(a2, b2)
        t, u = jnp.maximum(a2, b2), jnp.minimum(a4, b4)
        d2, d3 = order(t, u)
        m3, (m4, m5), m6 = jnp.maximum(d1, c2), order(d2, c3), jnp.minimum(d3, c4)
        for half, extra in ((0, 4 * group + 2), (1, 4 * group + 12)):
            mine = [w for w in wanted if (w - 4 * group - 1) // 2 == half]
            if not mine:
                continue
            p, q = pair(extra)
            s5 = jnp.minimum(m5, jnp.minimum(jnp.maximum(m4, p), jnp.maximum(m3, q)))
            s6 = jnp.minimum(m6, jnp.minimum(jnp.maximum(m5, p), jnp.maximum(m4, q)))
            for w in mine:
                lone = extra - 1 if (w - 4 * group - 1) == 0 else extra + 2 if (w - 4 * group - 1) == 3 else (
                    4 * group + 12 if half == 0 else 4 * group + 3
                )
                assert w <= lone <= w + 10 and lone < total
                result.append(jnp.maximum(s5, jnp.minimum(s6, values[lone])))
    assert len(result) == count
    return result


def clean_kernel(dims, start, shots_here, *refs):
    scalars, (left_ref, down_ref, up_ref, right_ref, out_ref, held), own, sems = refs[:3], refs[3:9], refs[9:12], refs[12]
    staged = [pltpu.make_async_copy(source, target, sems.at[i]) for i, (source, target) in enumerate(zip(scalars, own))]
    for copy in staged:
        copy.start()
    shifts_ref, low_ref, high_ref = own
    shots, chans, rows = dims
    first_shot = lax.axis_index("shot") * shots_here + start
    lead = 8
    for slot in range(2):
        for chan in range(chans):
            held[slot, chan, pl.ds(0, lead), :] = jnp.zeros((lead, LANES), jnp.float32)
    lane = lax.broadcasted_iota(jnp.int32, (rows, LANES), 1)

    def passes(shot, part):
        place = pl.ds(part * 8, 8)
        values = [left_ref[shot, i, place, :] for i in range(HALO)]
        values += [down_ref[shot, i, place, :] for i in range(HALO)]
        values += [up_ref[shot, i, place, :] for i in range(2 * HALO - chans, HALO)]
        values += [right_ref[shot, i, place, :] for i in range(HALO)]
        once = medians(values, chans + HALO)
        once = [values[HALF + i] - once[i] for i in range(chans + HALO)]
        twice = medians(once, chans)
        for i in range(chans):
            held[shot % 2, i, pl.ds(lead + part * 8, 8), :] = once[HALF + i] - twice[i]

    def restore(shot, chan):
        shift = shifts_ref[start + shot, chan]
        whole_rows, part = shift >> 7, shift & (LANES - 1)
        inside = (first_shot + shot >= low_ref[chan]) & (first_shot + shot < high_ref[chan])
        first = held[shot % 2, chan, pl.ds(lead - whole_rows, rows), :]
        second = held[shot % 2, chan, pl.ds(lead - 1 - whole_rows, rows), :]
        mixed = jnp.where(lane < LANES - part, first, second)
        moved = pltpu.roll(mixed, part, 1)
        out_ref[chan // 2, shot, chan % 2] = jnp.where(inside, moved, 0.0)

    parts = rows // 8
    for shot in range(shots + 1):
        for part in range(parts):
            if shot < shots:
                passes(shot, part)
            if shot > 0:
                if shot == 1 and part == 0:
                    for copy in staged:
                        copy.wait()
                for chan in range(part * chans // parts, (part + 1) * chans // parts):
                    restore(shot - 1, chan)


def clean(shifts, low, high, left, down, up, right, start, groups):
    shots, _, rows, _ = down.shape
    shots_here, chans = shifts.shape
    return pl.pallas_call(
        functools.partial(clean_kernel, (shots, chans, rows), start, shots_here),
        out_shape=jax.ShapeDtypeStruct((groups, shots, chans // groups, rows, LANES), jnp.float32),
        in_specs=[whole()] * 7,
        out_specs=whole(),
        scratch_shapes=[
            pltpu.VMEM((2, chans, 8 + rows, LANES), jnp.float32),
            *(pltpu.SMEM(one.shape, jnp.int32) for one in (shifts, low, high)),
            pltpu.SemaphoreType.DMA((3,)),
        ],
        compiler_params=pltpu.CompilerParams(vmem_limit_bytes=GRANT),
        name="clean",
    )(shifts, low, high, left, down, up, right)


def real_forward(x):
    n = len(x)
    if n == 1:
        return [(x[0], None)]
    if n == 2:
        return [(x[0] + x[1], None), (x[0] - x[1], None)]
    even, odd = real_forward(x[0::2]), real_forward(x[1::2])
    out = [None] * (n // 2 + 1)
    for k in range(n // 4 + 1):
        (er, ei), (or_, oi) = even[k], odd[k]
        if k == 0:
            out[0] = (er + or_, None)
            out[n // 2] = (er - or_, None)
        elif 4 * k == n:
            out[k] = (er, -or_)
        else:
            c, s = math_cos(k, n), math_sin(k, n)
            tr, ti = or_ * c + oi * s, oi * c - or_ * s
            out[k] = (er + tr, ei + ti)
            out[n // 2 - k] = (er - tr, ti - ei)
    return out


def real_backward(spectrum, n):
    if n == 1:
        return [spectrum[0][0]]
    if n == 2:
        return [spectrum[0][0] + spectrum[1][0], spectrum[0][0] - spectrum[1][0]]
    even, odd = [None] * (n // 4 + 1), [None] * (n // 4 + 1)
    for k in range(n // 4 + 1):
        (ar, ai), (br, bi) = spectrum[k], spectrum[n // 2 - k]
        if k == 0:
            even[0], odd[0] = (ar + br, None), (ar - br, None)
        elif 4 * k == n:
            even[k], odd[k] = (ar + ar, None), (-(ai + ai), None)
        else:
            c, s = math_cos(k, n), math_sin(k, n)
            even[k] = (ar + br, ai - bi)
            dr, di = ar - br, ai + bi
            odd[k] = (dr * c - di * s, di * c + dr * s)
    first, second = real_backward(even, n // 2), real_backward(odd, n // 2)
    return [v for both in zip(first, second) for v in both]


def math_cos(k, n):
    return float(np.float32(np.cos(2 * np.pi * k / n)))


def math_sin(k, n):
    return float(np.float32(np.sin(2 * np.pi * k / n)))


def split(x):
    top = x.astype(jnp.bfloat16)
    return top, (x - top.astype(jnp.float32)).astype(jnp.bfloat16)


def constant_split(x):
    x = np.asarray(x, np.float32)
    top = x.astype(jnp.bfloat16)
    return top, (x - top.astype(np.float32)).astype(jnp.bfloat16)


def tables(shots, rows):
    a = np.arange(rows)
    outer = 2 * np.pi * (np.outer(a, a) % rows) / rows
    b = np.arange(LANES)
    inner = 2 * np.pi * (np.outer(b, b) % LANES) / LANES
    turn = 2 * np.pi * np.outer(a, b) / (rows * LANES)
    c, s = np.cos(outer), np.sin(outer)
    outer_forward = np.block([[c, s], [-s, c]])
    outer_backward = np.block([[c, -s], [s, c]])
    c, s = np.cos(inner), np.sin(inner)
    inner_forward = np.block([[c, -s], [s, c]])
    inner_backward = np.block([[c, s], [-s, c]]) / (shots * rows * LANES)
    left = []
    for matrix in (outer_forward, outer_backward):
        top, rest = constant_split(matrix)
        left.append(jnp.asarray(np.concatenate([top, top, rest], axis=1)))
    right = []
    for matrix in (inner_forward, inner_backward):
        top, rest = constant_split(matrix)
        right.append(jnp.asarray(np.concatenate([top, top, rest], axis=0)))
    twist = jnp.asarray(np.stack([np.cos(turn), np.sin(turn)]), jnp.float32)
    return (*left, *right, twist)


def dot(a, b):
    return jnp.dot(a, b, preferred_element_type=jnp.float32)


def dip_kernel(dims, pieces, bands_ref, *refs):
    data_refs, refs = refs[: len(pieces)], refs[len(pieces) :]
    outer_f, outer_b, inner_f, inner_b, twist_ref, result_ref, held, out_ref, bands, band_sem, sems = refs
    shots, recs, rows = dims
    high = shots // 2
    band_copy = pltpu.make_async_copy(bands_ref, bands, band_sem)
    band_copy.start()
    first_rec = lax.axis_index("shot") * recs
    lane = lax.broadcasted_iota(jnp.int32, (rows, LANES), 1)
    frequency = lax.broadcasted_iota(jnp.int32, (rows, LANES), 0) + rows * lane
    distance = jnp.minimum(frequency, rows * LANES - frequency)

    for part in range(rows // 8):
        place, below = pl.ds(part * 8, 8), pl.ds(rows + part * 8, 8)
        for rec in range(recs):
            lanes = pl.ds(rec * LANES, LANES)
            gathered = [
                data_refs[piece][group, slot, rec, place, :]
                for group in range(shots // sum(pieces))
                for piece, count in enumerate(pieces)
                for slot in range(count)
            ]
            out = real_forward(gathered)
            for k in range(high + 1):
                re, im = out[k]
                held[k, place, lanes] = re
                if k > 0:
                    held[k, below, lanes] = jnp.zeros_like(re) if im is None else im

    def left_product(matrix, k):
        top, rest = split(held[k])
        return dot(matrix[...], jnp.concatenate([top, rest, top], axis=0))

    def right_product(lines, matrix):
        size = len(lines) // PARTS
        done = []
        for i in range(PARTS):
            top, rest = split(jnp.concatenate(lines[i * size : (i + 1) * size], axis=0))
            done.append(dot(jnp.concatenate([top, rest, top], axis=1), matrix[...]))
        return jnp.concatenate(done, axis=0)

    def some_waves(step):
        cos, sin = twist_ref[0], twist_ref[1]
        first = 1 + step * WAVES
        lines = []
        for i in range(WAVES):
            spec = left_product(outer_f, first + i)
            for rec in range(recs):
                mine = slice(rec * LANES, (rec + 1) * LANES)
                re, im = spec[:rows, mine], spec[rows:, mine]
                lines.append(jnp.concatenate([re * cos + im * sin, im * cos - re * sin], axis=1))
        wave = right_product(lines, inner_f)
        kept = []
        for i in range(WAVES):
            for rec in range(recs):
                n = (i * recs + rec) * rows
                keep = distance >= (first + i) * bands[first_rec + rec]
                kept.append(
                    jnp.concatenate(
                        [
                            jnp.where(keep, wave[n : n + rows, :LANES], 0.0),
                            jnp.where(keep, wave[n : n + rows, LANES:], 0.0),
                        ],
                        axis=1,
                    )
                )
        wave = right_product(kept, inner_b)
        for i in range(WAVES):
            for rec in range(recs):
                n = (i * recs + rec) * rows
                lanes = slice(rec * LANES, (rec + 1) * LANES)
                re, im = wave[n : n + rows, :LANES], wave[n : n + rows, LANES:]
                held[first + i, :rows, lanes] = re * cos - im * sin
                held[first + i, rows:, lanes] = im * cos + re * sin
        for i in range(WAVES):
            held[first + i] = left_product(outer_b, first + i)

    band_copy.wait()
    for step in range(high // WAVES):
        some_waves(step)

    copies = []
    for part in range(rows // 8):
        place, below = pl.ds(part * 8, 8), pl.ds(rows + part * 8, 8)
        for rec in range(recs):
            lanes = pl.ds(rec * LANES, LANES)
            spectrum = [(held[0, place, lanes] * (1.0 / shots), None)]
            for k in range(1, high + 1):
                spectrum.append((held[k, place, lanes], held[k, below, lanes] if k < high else None))
            back = real_backward(spectrum, shots)
            for shot in range(shots):
                out_ref[shot, pl.ds(part * (8 * recs) + rec, 8, stride=recs), :] = back[shot]
        done = pl.ds(part * (8 * recs), 8 * recs)
        copies.append(pltpu.make_async_copy(out_ref.at[:, done], result_ref.at[:, done], sems.at[part]))
        copies[-1].start()
    for copy in copies:
        copy.wait()


def dip_filter(gathered, dip_band):
    groups, _, recs, rows, _ = gathered[0].shape
    pieces = tuple(piece.shape[1] for piece in gathered)
    shots = groups * sum(pieces)
    out = pl.pallas_call(
        functools.partial(dip_kernel, (shots, recs, rows), pieces),
        out_shape=jax.ShapeDtypeStruct((shots, rows * recs, LANES), jnp.float32),
        in_specs=[whole(pltpu.HBM)] + [whole()] * (5 + len(gathered)),
        out_specs=whole(pltpu.HBM),
        scratch_shapes=[
            pltpu.VMEM((shots // 2 + 1, 2 * rows, recs * LANES), jnp.float32),
            pltpu.VMEM((shots, rows * recs, LANES), jnp.float32),
            pltpu.SMEM(dip_band.shape, jnp.int32),
            pltpu.SemaphoreType.DMA,
            pltpu.SemaphoreType.DMA((rows // 8,)),
        ],
        compiler_params=pltpu.CompilerParams(vmem_limit_bytes=GRANT),
        name="dip",
    )(pltpu.with_memory_space_constraint(dip_band, pltpu.HBM), *gathered, *tables(shots, rows))
    return out.reshape(shots, rows, recs, LANES).transpose(0, 2, 1, 3).reshape(shots, recs, rows * LANES)


def local(traces, shifts, aperture_lo, aperture_hi, dip_band):
    blocks, groups = lax.axis_size("chan"), lax.axis_size("shot")
    upward, downward = [(i, i + 1) for i in range(blocks - 1)], [(i + 1, i) for i in range(blocks - 1)]
    edges = align(traces, shifts, PIECES)
    sides = []
    for i in range(len(PIECES)):
        down, up = edges[2 * i : 2 * i + 2]
        left = lax.ppermute(up, "chan", upward)
        right = lax.ppermute(down, "chan", downward)
        sides.append((left, down, up, right))
    arrived = []
    for i in range(len(PIECES)):
        parted = clean(shifts, aperture_lo, aperture_hi, *sides[i], sum(PIECES[:i]), groups)
        arrived.append(lax.all_to_all(parted, "shot", split_axis=0, concat_axis=0, tiled=True))
    return dip_filter(arrived, dip_band)


def solution(mesh):
    return jax.shard_map(
        local,
        mesh=mesh,
        in_specs=(P("shot", "chan", None), P("shot", "chan"), P("chan"), P("chan"), P("chan")),
        out_specs=P(None, ("chan", "shot"), None),
        check_vma=False,
    )
```
